512 devices in a mesh: gx: 32 (over z, core), gy: 16 (over y, x).
Axes of the slice: x: 4, y: 4, z: 16, core: 2. Of those that a mesh axis runs over, the one named last changes fastest.
Arguments:
- field: float32 [1024, 512, 256], P('gx', 'gy'), may hold values from -192 to 192
- cond_x: float32 [1024, 512, 256], P('gx', 'gy'), may hold values from 1 to 4
- cond_y: float32 [1024, 512, 256], P('gx', 'gy'), may hold values from 1 to 4
- cross_weight: float32 [1024, 512, 256], P('gx', 'gy'), may hold values from -4 to 4
Outputs:
- field_next: float32 [1024, 512, 256], P('gx', 'gy')
The draws below stay inside these ranges and needn't reach their ends.
All inputs are finite; a program needn't handle non-finite values.
Results may differ from the reference program's by a relative error of at most 0.0007.
Values sent between devices are 32-bit elements; how exact they have to be, the bound alone decides.
No kernel may reach another device: no remote copies, remote signals or barrier semaphores. Data moves between devices by JAX's collectives and lax.ppermute only.
A program may use at most 64 MiB of HBM per device.

```python
import math
import jax
import jax.numpy as jnp
from jax import lax

NZ = 256
NX = 1024
NY = 512


def draw_field(key, part):
    values = 32.0 * jax.random.normal(key, (NX, NY, NZ), jnp.float32)
    return jnp.clip(values, -192.0, 192.0)


def block_scale(rng, extent, cuts, low, high):
    loudness = 1.0
    for axis_at, shards_of in cuts:
        draws = jax.random.uniform(jax.random.fold_in(jax.random.fold_in(rng, 6), axis_at), (shards_of,), jnp.float32, low / len(cuts), high / len(cuts))
        loudness = loudness * jnp.repeat(jnp.exp(draws), extent[axis_at] // shards_of).reshape((-1,) + (1,) * (len(extent) - 1 - axis_at))
    return loudness


def setup_inputs(seed: int = 0) -> dict:
    keys = jax.random.split(jax.random.key(seed), 5)
    return {
        "field": draw_field(jax.random.fold_in(keys[4], 71), 0),
        "cond_x": jnp.clip(jnp.exp(math.log(4.0) - 1.3862944 * jax.random.uniform(keys[1], (NX, NY, NZ), jnp.float32) ** block_scale(keys[1], (NX, NY, NZ), ((0, 32), (1, 16)), -0.2, 0.2)), 1.0, 4.0),
        "cond_y": jnp.clip(jnp.exp(math.log(4.0) - 1.3862944 * jax.random.uniform(keys[2], (NX, NY, NZ), jnp.float32) ** block_scale(keys[2], (NX, NY, NZ), ((0, 32), (1, 16)), -0.2, 0.2)), 1.0, 4.0),
        "cross_weight": jnp.clip(jax.random.uniform(keys[3], (NX, NY, NZ), jnp.float32, -4.0, 4.0) * block_scale(keys[3], (NX, NY, NZ), ((0, 32), (1, 16)), -0.4, 0.0), -4.0, 4.0),
    }


step_dt = 16384.0


def thomas(lower_band, center, upper_band, right_side):
    def forward(carry, items):
        prev_ratio, prev_value = carry
        below_term, middle, above_term, right_term = items
        denominator = middle - below_term * prev_ratio
        next_ratio = above_term / denominator
        next_value = (right_term - below_term * prev_value) / denominator
        return (next_ratio, next_value), (next_ratio, next_value)

    start = (jnp.zeros_like(center[0]), jnp.zeros_like(right_side[0]))
    leftover, (ratios, values) = lax.scan(forward, start, (lower_band, center, upper_band, right_side))

    def backward(after, items):
        ratio, value = items
        here = value - ratio * after
        return here, here

    remaining, result = lax.scan(backward, jnp.zeros_like(right_side[0]), (ratios, values), reverse=True)
    return result


def line_solve(coef, right_side):
    following = jnp.concatenate([coef[1:], jnp.zeros_like(coef[:1])], axis=0)
    lower_band = -step_dt * coef
    upper_band = -step_dt * following
    center = 1.0 + step_dt * (coef + following)
    return thomas(lower_band, center, upper_band, right_side)


def reference(field, cond_x, cond_y, cross_weight):
    padded = jnp.pad(field, ((1, 1), (1, 1), (0, 0)))
    mixed = padded[2:, 2:] - padded[2:, :-2] - padded[:-2, 2:] + padded[:-2, :-2]
    source = field + cross_weight * mixed * 0.25
    half = line_solve(cond_x, source)
    turned = line_solve(jnp.moveaxis(cond_y, 1, 0), jnp.moveaxis(half, 1, 0))
    return jnp.moveaxis(turned, 1, 0)
```

```python
import functools

import jax
import jax.numpy as jnp
from jax import lax
from jax.experimental import pallas as pl
from jax.experimental.pallas import tpu as pltpu
from jax.sharding import PartitionSpec as P

STEP = 16384.0
LANES = 128
SUB = 8
VALUES = 5
MIB = 1 << 20
f32 = jnp.float32


def tile_view(x):
    nx, ny, nz = x.shape
    x = x.reshape(nx, ny // SUB, SUB, nz // LANES, LANES)
    return x.transpose(0, 1, 3, 2, 4).reshape(nx * ny * nz // LANES, LANES)


def from_tile_view(v, shape):
    nx, ny, nz = shape
    v = v.reshape(nx, ny // SUB, nz // LANES, SUB, LANES)
    return v.transpose(0, 1, 3, 2, 4).reshape(nx, ny, nz)


def y_rows(shape, y, half):
    nx, ny, nz = shape
    halves = nz // LANES
    start = ((y // SUB) * halves + half) * SUB + y % SUB
    return pl.ds(start, nx, stride=ny * halves)


def load_y(ref, shape, y):
    parts = [ref[y_rows(shape, y, h), :] for h in range(shape[2] // LANES)]
    return jnp.concatenate(parts, axis=1)


def store_y(ref, shape, y, value):
    for h in range(shape[2] // LANES):
        ref[y_rows(shape, y, h), :] = value[:, h * LANES : (h + 1) * LANES]


def store_plane(ref, shape, x, value):
    nx, ny, nz = shape
    halves = nz // LANES
    for yb in range(ny // SUB):
        for h in range(halves):
            start = ((x * (ny // SUB) + yb) * halves + h) * SUB
            ref[start : start + SUB, :] = value[
                yb * SUB : (yb + 1) * SUB, h * LANES : (h + 1) * LANES
            ]


def store_values(ref, values):
    lines, width = values[0].shape
    halves = width // LANES
    for k, value in enumerate(values):
        for h in range(halves):
            ref[pl.ds(k * halves + h, lines, stride=len(values) * halves), :] = value[
                :, h * LANES : (h + 1) * LANES
            ]


def load_values(ref, lines, count, halves):
    return [
        jnp.concatenate(
            [ref[pl.ds(k * halves + h, lines, stride=count * halves), :] for h in range(halves)],
            axis=1,
        )
        for k in range(count)
    ]


def eliminate(face, n, inv_ref, gam_ref, tau_ref, mat_ref):
    t = STEP * face(0)
    a = jnp.zeros_like(t)
    ground = jnp.ones_like(t)
    for i in range(n - 1):
        c = STEP * face(i + 1)
        inv = 1.0 / (t + ground + c)
        gam = c * inv
        tau = t * inv
        inv_ref[i] = inv
        gam_ref[i] = gam
        tau_ref[i] = tau
        a = a + tau * ground
        ground = 1.0 + gam * ground
        t = t * gam
    mat_ref[0] = t
    mat_ref[1] = a
    mat_ref[2] = ground


def matrix_x_kernel(c_ref, inv_ref, gam_ref, tau_ref, mat_ref):
    eliminate(lambda i: c_ref[i], c_ref.shape[0], inv_ref, gam_ref, tau_ref, mat_ref)


def matrix_y_kernel(shape, c_ref, inv_ref, gam_ref, tau_ref, mat_ref):
    eliminate(lambda y: load_y(c_ref, shape, y), shape[1], inv_ref, gam_ref, tau_ref, mat_ref)


def y_difference(plane, below, above):
    n = plane.shape[0]
    row = lax.broadcasted_iota(jnp.int32, plane.shape, 0)
    up = jnp.where(row == n - 1, above, pltpu.roll(plane, n - 1, 0))
    down = jnp.where(row == 0, below, pltpu.roll(plane, 1, 0))
    return up - down


def rim_kernel(first_ref, last_ref, below_ref, above_ref, d_first_ref, d_last_ref):
    n = below_ref.shape[0]
    d_first_ref[...] = y_difference(first_ref[0], below_ref[0:1, :], above_ref[0:1, :])
    d_last_ref[...] = y_difference(last_ref[0], below_ref[n - 1 : n, :], above_ref[n - 1 : n, :])


def forward(source, n, inv_ref, gam_ref, tau_ref, mat_ref, phi_ref, buf_ref):
    q = None
    j = None
    for i in range(n - 1):
        h = source(i) if q is None else source(i) + q
        phi_ref[i] = inv_ref[i] * h
        q = gam_ref[i] * h
        j = tau_ref[i] * h if j is None else j + tau_ref[i] * h
    q = q + source(n - 1)
    store_values(buf_ref, [mat_ref[0], mat_ref[1], mat_ref[2], j, q])


def backward(n, u_prev, u_own, gam_ref, tau_ref, phi_ref, emit):
    u = u_own
    emit(n - 1, u)
    for i in range(n - 2, -1, -1):
        u = phi_ref[i] + tau_ref[i] * u_prev + gam_ref[i] * u
        emit(i, u)


def forward_x_kernel(
    field_ref, weight_ref, below_ref, above_ref, dm_ref, dp_ref,
    inv_ref, gam_ref, tau_ref, mat_ref, phi_ref, buf_ref,
):
    n = field_ref.shape[0]

    def diff(i):
        if i < 0:
            return dm_ref[...]
        if i >= n:
            return dp_ref[...]
        return y_difference(field_ref[i], below_ref[i : i + 1, :], above_ref[i : i + 1, :])

    diffs = {}

    def source(i):
        for k in (i - 1, i, i + 1):
            if k not in diffs:
                diffs[k] = diff(k)
        mixed = diffs[i + 1] - diffs.pop(i - 1)
        return field_ref[i] + weight_ref[i] * mixed * 0.25

    forward(source, n, inv_ref, gam_ref, tau_ref, mat_ref, phi_ref, buf_ref)


def solve_kernel(n, m, halves, in_ref, out_ref):
    stride = m * VALUES * halves

    def get(k):
        return jnp.concatenate(
            [
                in_ref[pl.ds((l * VALUES + k) * halves + h, n, stride=stride), :]
                for l in range(m)
                for h in range(halves)
            ],
            axis=1,
        )

    t, a, ground, j, q = (get(k) for k in range(VALUES))
    row = lax.broadcasted_iota(jnp.int32, t.shape, 0)
    first = row == 0
    last = row == n - 1

    def after(v, d=1):
        return pltpu.roll(v, n - d, 0)

    def before(v, d=1):
        return pltpu.roll(v, d, 0)

    g = ground + jnp.where(last, 0.0, after(a)) + jnp.where(first, t, 0.0)
    low = jnp.where(first, 0.0, t)
    high = jnp.where(last, 0.0, after(t))
    r = q + jnp.where(last, 0.0, after(j))
    d = 1
    while d < n:
        inv = 1.0 / (g + low + high)
        gi = g * inv
        ri = r * inv
        g, r, low, high = (
            g + low * before(gi, d) + high * after(gi, d),
            r + low * before(ri, d) + high * after(ri, d),
            low * before(low * inv, d),
            high * after(high * inv, d),
        )
        d *= 2
    u = r / g
    u_prev = jnp.where(first, 0.0, before(u))
    for l in range(m):
        for k, value in enumerate((u_prev, u)):
            for h in range(halves):
                at = (l * halves + h) * LANES
                out_ref[pl.ds((l * 2 + k) * halves + h, n, stride=m * 2 * halves), :] = value[
                    :, at : at + LANES
                ]


def middle_kernel(
    shape, ends_ref, phi_x_ref, gam_x_ref, tau_x_ref, inv_ref, gam_ref, tau_ref, mat_ref,
    phi_ref, buf_ref, half_ref,
):
    nx, ny, nz = shape
    u_prev, u_own = load_values(ends_ref, ny, 2, nz // LANES)
    backward(nx, u_prev, u_own, gam_x_ref, tau_x_ref, phi_x_ref,
             lambda i, u: store_plane(half_ref, shape, i, u))
    forward(lambda y: load_y(half_ref, shape, y), ny, inv_ref, gam_ref, tau_ref, mat_ref, phi_ref, buf_ref)


def backward_y_kernel(shape, ends_ref, phi_ref, gam_ref, tau_ref, out_ref):
    nx, ny, nz = shape
    u_prev, u_own = load_values(ends_ref, nx, 2, nz // LANES)
    backward(ny, u_prev, u_own, gam_ref, tau_ref, phi_ref,
             lambda y, u: store_y(out_ref, shape, y, u))


def vmem(count):
    return [pl.BlockSpec(memory_space=pltpu.VMEM)] * count


def call(kernel, args, outs, name, scratch=(), cost=(1000, 1 << 20), in_specs=None):
    return pl.pallas_call(
        kernel,
        out_shape=[jax.ShapeDtypeStruct(s, f32) for s in outs],
        in_specs=vmem(len(args)) if in_specs is None else in_specs,
        out_specs=vmem(len(outs)),
        scratch_shapes=[pltpu.VMEM(s, f32) for s in scratch],
        compiler_params=pltpu.CompilerParams(vmem_limit_bytes=16 * MIB),
        cost_estimate=pl.CostEstimate(flops=cost[0], bytes_accessed=cost[1], transcendentals=0),
        name=name,
    )(*args)


def shift(value, axis, up):
    count = lax.axis_size(axis)
    pairs = [(i, i + 1) for i in range(count - 1)]
    return lax.ppermute(value, axis, pairs if up else [(j, i) for i, j in pairs])


def exchange(buf, axis):
    n = lax.axis_size(axis)
    rows, lanes = buf.shape
    got = lax.all_to_all(buf.reshape(n, 1, rows * lanes // n), axis, 0, 0, tiled=True)
    return got.reshape(rows, lanes)


def interfaces(buf, axis, lines, halves):
    n = lax.axis_size(axis)
    m = lines // n
    every = exchange(buf, axis)
    kernel = functools.partial(solve_kernel, n, m, halves)
    (ends,) = call(kernel, [every], [(n * m * 2 * halves, LANES)], "solve_" + axis)
    return exchange(ends, axis)


def shards(field, cond_x, cond_y, cross_weight):
    shape = nx, ny, nz = field.shape
    halves = nz // LANES
    below = shift(field[:, ny - 1, :], "gy", True)
    above = shift(field[:, 0, :], "gy", False)
    x_plane = (ny, nz)
    y_plane = (nx, nz)
    matrix_x = call(
        matrix_x_kernel, [cond_x], [(nx, *x_plane)] * 3 + [(3, *x_plane)], "matrix_x"
    )
    matrix_y = call(
        functools.partial(matrix_y_kernel, shape), [tile_view(cond_y)],
        [(ny, *y_plane)] * 3 + [(3, *y_plane)], "matrix_y",
    )
    d_first, d_last = call(
        rim_kernel, [field[:1], field[nx - 1 :], below, above], [x_plane] * 2, "rim"
    )
    d_before = shift(d_last, "gx", True)
    d_after = shift(d_first, "gx", False)
    phi_x, buf_x = call(
        forward_x_kernel,
        [field, cross_weight, below, above, d_before, d_after, *matrix_x],
        [(nx, *x_plane), (ny * VALUES * halves, LANES)],
        "forward_x",
    )
    ends_x = interfaces(buf_x, "gx", ny, halves)
    phi_y, buf_y = call(
        functools.partial(middle_kernel, shape),
        [ends_x, phi_x, matrix_x[1], matrix_x[2], *matrix_y],
        [(ny, *y_plane), (nx * VALUES * halves, LANES)],
        "middle",
        scratch=[(nx * ny * halves, LANES)],
    )
    ends_y = interfaces(buf_y, "gy", nx, halves)
    (out,) = call(
        functools.partial(backward_y_kernel, shape),
        [ends_y, phi_y, matrix_y[1], matrix_y[2]],
        [(nx * ny * halves, LANES)],
        "backward_y",
    )
    return from_tile_view(out, shape)


def solution(mesh):
    spec = P("gx", "gy", None)
    return jax.shard_map(
        shards, mesh=mesh, in_specs=(spec,) * 4, out_specs=spec, check_vma=False
    )
```

```python
import functools

import jax
import jax.numpy as jnp
from jax import lax
from jax.experimental import pallas as pl
from jax.experimental.pallas import tpu as pltpu
from jax.sharding import PartitionSpec as P

STEP = 16384.0
LANES = 128
SUB = 8
MIB = 1 << 20
f32 = jnp.float32


def tile_rows(x):
    nx, ny, nz = x.shape
    x = x.reshape(nx, ny // SUB, SUB, nz // LANES, LANES)
    return x.transpose(0, 1, 3, 2, 4).reshape(nx * ny * nz // LANES, LANES)


def from_y_blocks(v, shape):
    nx, ny, nz = shape
    v = v.reshape(nx, ny // SUB, nz // LANES, SUB, LANES)
    return v.transpose(0, 1, 3, 2, 4).reshape(nx, ny, nz)


def y_scratch(shape):
    nx, ny, nz = shape
    return pltpu.VMEM((ny // SUB, nx * nz * SUB // LANES, LANES), f32)


def y_rows(shape, y, h):
    nx, _, nz = shape
    return y // SUB, pl.ds(h * SUB + y % SUB, nx, stride=SUB * nz // LANES), slice(None)


def load_y(ref, shape, y):
    return jnp.concatenate([ref[y_rows(shape, y, h)] for h in range(shape[2] // LANES)], axis=1)


def load_y_whole(ref, shape, y):
    nx, ny, nz = shape
    at = y // SUB * SUB * (nz // LANES) + y % SUB
    parts = [
        ref[pl.ds(at + h * SUB, nx, stride=ny * nz // LANES), :] for h in range(nz // LANES)
    ]
    return jnp.concatenate(parts, axis=1)


def store_y(ref, shape, y, value):
    for h in range(shape[2] // LANES):
        ref[y_rows(shape, y, h)] = value[:, h * LANES : (h + 1) * LANES]


def store_plane(ref, shape, x, value):
    _, ny, nz = shape
    halves = nz // LANES
    for yb in range(ny // SUB):
        for h in range(halves):
            start = (x * halves + h) * SUB
            ref[yb, start : start + SUB, :] = value[
                yb * SUB : (yb + 1) * SUB, h * LANES : (h + 1) * LANES
            ]


def y_block_out(scratch, hbm, yb, sem):
    block = scratch.at[yb].reshape(hbm.shape[0], hbm.shape[2], LANES)
    return pltpu.make_async_copy(block, hbm.at[:, yb], sem.at[yb])


def store_values(ref, values):
    lines, width = values[0].shape
    halves = width // LANES
    for k, value in enumerate(values):
        for h in range(halves):
            ref[pl.ds(k * halves + h, lines, stride=len(values) * halves), :] = value[
                :, h * LANES : (h + 1) * LANES
            ]


def load_values(ref, lines, count, halves):
    return [
        jnp.concatenate(
            [ref[pl.ds(k * halves + h, lines, stride=count * halves), :] for h in range(halves)],
            axis=1,
        )
        for k in range(count)
    ]


def matrix_x_kernel(c_ref, inv_ref, gam_ref, tau_ref, mat_ref):
    n = c_ref.shape[0]
    left = STEP * c_ref[0]
    t = left
    a = jnp.zeros_like(t)
    ground = jnp.ones_like(t)
    for i in range(n - 1):
        c = STEP * c_ref[i + 1]
        inv = 1.0 / (t + ground + c)
        gam = c * inv
        tau = t * inv
        inv_ref[i] = inv
        gam_ref[i] = gam
        tau_ref[i] = tau
        a = a + tau * ground
        ground = 1.0 + gam * ground
        t = t * gam
    for k, value in enumerate((t, a, ground, left)):
        mat_ref[k] = value


def y_difference(plane, below, above):
    n = plane.shape[0]
    row = lax.broadcasted_iota(jnp.int32, plane.shape, 0)
    up = jnp.where(row == n - 1, above, pltpu.roll(plane, n - 1, 0))
    down = jnp.where(row == 0, below, pltpu.roll(plane, 1, 0))
    return up - down


def rim_kernel(field_ref, below_ref, above_ref, mat_ref, up_ref, down_ref):
    n = field_ref.shape[0]
    ny = field_ref.shape[1]
    up_ref[...] = y_difference(field_ref[n - 1], below_ref[n - 1 : n, :], above_ref[n - 1 : n, :])
    down_ref[0:ny, :] = y_difference(field_ref[0], below_ref[0:1, :], above_ref[0:1, :])
    down_ref[ny:, :] = mat_ref[1]


def forward_x_kernel(
    field_ref, weight_ref, below_ref, above_ref, inv_ref, gam_ref, tau_ref, phi_ref, side_ref,
):
    n = field_ref.shape[0]
    diffs = {}

    def diff(i):
        if not 0 <= i < n:
            return 0.0
        if i not in diffs:
            diffs[i] = y_difference(field_ref[i], below_ref[i : i + 1, :], above_ref[i : i + 1, :])
        return diffs[i]

    q = j = 0.0
    for i in range(n):
        mixed = diff(i + 1) - diff(i - 1)
        diffs.pop(i - 1, None)
        h = field_ref[i] + weight_ref[i] * mixed * 0.25 + q
        if i < n - 1:
            phi_ref[i] = inv_ref[i] * h
            q = gam_ref[i] * h
            j = j + tau_ref[i] * h
    for k, value in enumerate((j, h, weight_ref[0] * 0.25, weight_ref[n - 1] * 0.25)):
        side_ref[k] = value


def finish_x_kernel(before_ref, after_ref, mat_ref, side_ref, buf_ref, extra_ref):
    ny = before_ref.shape[0]
    t, a, ground, left = (mat_ref[k] for k in range(4))
    f0 = -side_ref[2] * before_ref[...]
    extra = f0 / left
    j = side_ref[0] + f0 - (a + t) * extra
    q = side_ref[1] + t * extra + side_ref[3] * after_ref[0:ny, :]
    extra_ref[...] = extra
    store_values(buf_ref, [t, ground + after_ref[ny:, :], j, q])


def solve_kernel(n, m, halves, count, in_ref, out_ref):
    stride = m * count * halves

    def get(k):
        return jnp.concatenate(
            [
                in_ref[pl.ds((l * count + k) * halves + h, n, stride=stride), :]
                for l in range(m)
                for h in range(halves)
            ],
            axis=1,
        )

    t, g, j, q, *a = (get(k) for k in range(count))
    row = lax.broadcasted_iota(jnp.int32, t.shape, 0)
    first = row == 0
    last = row == n - 1

    def after(v, d=1):
        return pltpu.roll(v, n - d, 0)

    def before(v, d=1):
        return pltpu.roll(v, d, 0)

    g = g + jnp.where(first, t, 0.0)
    if a:
        g = g + jnp.where(last, 0.0, after(a[0]))
    low = jnp.where(first, 0.0, t)
    high = jnp.where(last, 0.0, after(t))
    r = q + jnp.where(last, 0.0, after(j))
    d = 1
    while d < n:
        inv = 1.0 / (g + low + high)
        gi = g * inv
        ri = r * inv
        g, r, low, high = (
            g + low * before(gi, d) + high * after(gi, d),
            r + low * before(ri, d) + high * after(ri, d),
            low * before(low * inv, d),
            high * after(high * inv, d),
        )
        d *= 2
    u = r / g
    u_prev = jnp.where(first, 0.0, before(u))
    for l in range(m):
        for k, value in enumerate((u_prev, u)):
            for h in range(halves):
                at = (l * halves + h) * LANES
                out_ref[pl.ds((l * 2 + k) * halves + h, n, stride=m * 2 * halves), :] = value[
                    :, at : at + LANES
                ]


def backward(n, u_prev, u_own, gam_ref, tau_ref, phi_ref, emit):
    u = u_own
    emit(n - 1, u)
    for i in range(n - 2, -1, -1):
        u = (phi_ref[i] + tau_ref[i] * u_prev) + gam_ref[i] * u
        emit(i, u)


def middle_kernel(
    shape, ends_ref, extra_ref, phi_x_ref, gam_x_ref, tau_x_ref, c_ref,
    phi_ref, gam_ref, tau_ref, buf_ref, half_ref,
):
    nx, ny, nz = shape
    u_prev, u_own = load_values(ends_ref, ny, 2, nz // LANES)
    backward(nx, u_prev + extra_ref[...], u_own, gam_x_ref, tau_x_ref, phi_x_ref,
             lambda i, u: store_plane(half_ref, shape, i, u))
    t = STEP * load_y_whole(c_ref, shape, 0)
    a = jnp.zeros_like(t)
    ground = jnp.ones_like(t)
    q = j = 0.0
    for y in range(ny - 1):
        c = STEP * load_y_whole(c_ref, shape, y + 1)
        h = load_y(half_ref, shape, y) + q
        inv = 1.0 / (t + ground + c)
        gam = c * inv
        tau = t * inv
        phi_ref[y] = inv * h
        gam_ref[y] = gam
        tau_ref[y] = tau
        q = gam * h
        j = j + tau * h
        a = a + tau * ground
        ground = 1.0 + gam * ground
        t = t * gam
    q = q + load_y(half_ref, shape, ny - 1)
    store_values(buf_ref, [t, ground, j, q, a])


def backward_y_kernel(shape, ends_ref, phi_ref, gam_ref, tau_ref, out_hbm, out_ref, sem):
    nx, ny, nz = shape
    u_prev, u_own = load_values(ends_ref, nx, 2, nz // LANES)
    copies = []

    def emit(y, u):
        store_y(out_ref, shape, y, u)
        if y % SUB == 0:
            copies.append(y_block_out(out_ref, out_hbm, y // SUB, sem))
            copies[-1].start()

    backward(ny, u_prev, u_own, gam_ref, tau_ref, phi_ref, emit)
    for copy in copies:
        copy.wait()


IN_VMEM = pl.BlockSpec(memory_space=pltpu.VMEM)
IN_HBM = pl.BlockSpec(memory_space=pltpu.HBM)


def call(kernel, args, outs, name, scratch=(), hbm_outs=(), bytes_accessed=1 << 20):
    return pl.pallas_call(
        kernel,
        out_shape=[jax.ShapeDtypeStruct(s, f32) for s in outs],
        in_specs=[IN_VMEM] * len(args),
        out_specs=[IN_HBM if k in hbm_outs else IN_VMEM for k in range(len(outs))],
        scratch_shapes=list(scratch),
        compiler_params=pltpu.CompilerParams(vmem_limit_bytes=16 * MIB),
        cost_estimate=pl.CostEstimate(flops=1 << 20, bytes_accessed=bytes_accessed, transcendentals=0),
        name=name,
    )(*args)


def shift(value, axis, up):
    count = lax.axis_size(axis)
    pairs = [(i, i + 1) for i in range(count - 1)]
    return lax.ppermute(value, axis, pairs if up else [(j, i) for i, j in pairs])


def exchange(buf, axis):
    n = lax.axis_size(axis)
    rows, lanes = buf.shape
    got = lax.all_to_all(buf.reshape(n, 1, rows * lanes // n), axis, 0, 0, tiled=True)
    return got.reshape(rows, lanes)


def interfaces(buf, axis, lines, halves, count):
    n = lax.axis_size(axis)
    m = lines // n
    every = exchange(buf, axis)
    kernel = functools.partial(solve_kernel, n, m, halves, count)
    (ends,) = call(kernel, [every], [(n * m * 2 * halves, LANES)], "solve_" + axis)
    return exchange(ends, axis)


def shards(field, cond_x, cond_y, cross_weight):
    shape = nx, ny, nz = field.shape
    halves = nz // LANES
    x_plane = (ny, nz)
    y_plane = (nx, nz)
    blocks = pltpu.SemaphoreType.DMA((ny // SUB,))
    below = shift(field[:, ny - 1, :], "gy", True)
    above = shift(field[:, 0, :], "gy", False)
    inv_x, gam_x, tau_x, mat_x = call(
        matrix_x_kernel, [cond_x], [(nx - 1, *x_plane)] * 3 + [(4, *x_plane)], "matrix_x",
        bytes_accessed=4 << 20,
    )
    up, down = call(
        rim_kernel, [field, below, above, mat_x], [x_plane, (2 * ny, nz)], "rim"
    )
    before = shift(up, "gx", True)
    after = shift(down, "gx", False)
    phi_x, side = call(
        forward_x_kernel, [field, cross_weight, below, above, inv_x, gam_x, tau_x],
        [(nx - 1, *x_plane), (4, *x_plane)], "forward_x",
        bytes_accessed=4 << 20,
    )
    buf_x, extra = call(
        finish_x_kernel, [before, after, mat_x, side], [(ny * 4 * halves, LANES), x_plane], "finish_x"
    )
    ends_x = interfaces(buf_x, "gx", ny, halves, 4)
    phi_y, gam_y, tau_y, buf_y = call(
        functools.partial(middle_kernel, shape),
        [ends_x, extra, phi_x, gam_x, tau_x, tile_rows(cond_y)],
        [(ny - 1, *y_plane)] * 3 + [(nx * 5 * halves, LANES)], "middle",
        scratch=(y_scratch(shape),),
    )
    ends_y = interfaces(buf_y, "gy", nx, halves, 5)
    (out,) = call(
        functools.partial(backward_y_kernel, shape), [ends_y, phi_y, gam_y, tau_y],
        [(nx, ny // SUB, SUB * halves, LANES)], "backward_y",
        scratch=(y_scratch(shape), blocks), hbm_outs=(0,),
    )
    return from_y_blocks(out, shape)


def solution(mesh):
    spec = P("gx", "gy", None)
    return jax.shard_map(
        shards, mesh=mesh, in_specs=(spec,) * 4, out_specs=spec, check_vma=False
    )
```

```python
import functools

import jax
import jax.numpy as jnp
from jax import lax
from jax.experimental import pallas as pl
from jax.experimental.pallas import tpu as pltpu
from jax.sharding import PartitionSpec as P

STEP = 16384.0
LANES = 128
SUB = 8
MIB = 1 << 20
MOST_VMEM = 66322432
f32 = jnp.float32


def tile_rows(x):
    nx, ny, nz = x.shape
    x = x.reshape(nx, ny // SUB, SUB, nz // LANES, LANES)
    return x.transpose(0, 1, 3, 2, 4).reshape(nx * ny * nz // LANES, LANES)


def from_y_blocks(v, shape):
    nx, ny, nz = shape
    v = v.reshape(nx, ny // SUB, nz // LANES, SUB, LANES)
    return v.transpose(0, 1, 3, 2, 4).reshape(nx, ny, nz)


def y_scratch(shape):
    nx, ny, nz = shape
    return pltpu.VMEM((ny // SUB, nx * nz * SUB // LANES, LANES), f32)


def y_rows(shape, y, h):
    nx, _, nz = shape
    return y // SUB, pl.ds(h * SUB + y % SUB, nx, stride=SUB * nz // LANES), slice(None)


def load_y(ref, shape, y):
    return jnp.concatenate([ref[y_rows(shape, y, h)] for h in range(shape[2] // LANES)], axis=1)


def load_y_whole(ref, shape, y):
    nx, ny, nz = shape
    at = y // SUB * SUB * (nz // LANES) + y % SUB
    parts = [
        ref[pl.ds(at + h * SUB, nx, stride=ny * nz // LANES), :] for h in range(nz // LANES)
    ]
    return jnp.concatenate(parts, axis=1)


def store_y(ref, shape, y, value):
    for h in range(shape[2] // LANES):
        ref[y_rows(shape, y, h)] = value[:, h * LANES : (h + 1) * LANES]


def store_plane(ref, shape, x, value):
    _, ny, nz = shape
    halves = nz // LANES
    for yb in range(ny // SUB):
        for h in range(halves):
            start = (x * halves + h) * SUB
            ref[yb, start : start + SUB, :] = value[
                yb * SUB : (yb + 1) * SUB, h * LANES : (h + 1) * LANES
            ]


def y_block_out(scratch, hbm, yb, sem):
    block = scratch.at[yb].reshape(hbm.shape[0], hbm.shape[2], LANES)
    return pltpu.make_async_copy(block, hbm.at[:, yb], sem.at[yb])


def store_values(ref, values):
    lines, width = values[0].shape
    halves = width // LANES
    for k, value in enumerate(values):
        for h in range(halves):
            ref[pl.ds(k * halves + h, lines, stride=len(values) * halves), :] = value[
                :, h * LANES : (h + 1) * LANES
            ]


def load_values(ref, lines, count, halves):
    return [
        jnp.concatenate(
            [ref[pl.ds(k * halves + h, lines, stride=count * halves), :] for h in range(halves)],
            axis=1,
        )
        for k in range(count)
    ]


def pack_kernel(field_hbm, weight_hbm, c_hbm, rows_ref, field_ref, weight_ref, c_ref, sem):
    tile = pl.ds(field_hbm.shape[1] - SUB, SUB)
    copies = [
        pltpu.make_async_copy(hbm.at[:, tile, :], ref, sem.at[k])
        for k, (hbm, ref) in enumerate(
            ((field_hbm, field_ref), (weight_hbm, weight_ref), (c_hbm, c_ref))
        )
    ]
    for copy in copies:
        copy.start()
    for copy in copies:
        copy.wait()
    rows_ref[0] = field_ref[:, SUB - 1, :]
    rows_ref[1] = field_ref[:, SUB - 2, :]
    rows_ref[2] = weight_ref[:, SUB - 1, :]
    rows_ref[3] = c_ref[:, SUB - 1, :]


def stage_kernel(field_ref, weight_ref, c_ref, token_ref):
    token_ref[...] = field_ref[0, 0:SUB, 0:LANES] + weight_ref[0, 0:SUB, 0:LANES] + c_ref[0, 0:SUB, 0:LANES]


def not_first(axis):
    return jnp.where(lax.axis_index(axis) == 0, 0.0, 1.0).astype(f32)


class Rows:
    def __init__(self, shape, rows_ref, inside):
        self.n = shape[0]
        self.row = lax.broadcasted_iota(jnp.int32, shape, 0)
        self.rows_ref = rows_ref
        self.inside = inside

    def put(self, place, row, plane):
        return jnp.where(self.row == place, row, plane)

    def got(self, k, i):
        return self.rows_ref[k, i : i + 1, :]

    def plane(self, ref, k, i):
        return self.put(self.n - 1, self.got(k, i), ref[i])

    def difference(self, ref, i):
        n = self.n
        plane = ref[i]
        up = pltpu.roll(plane, n - 1, 0)
        up = self.put(n - 1, up * self.inside, up)
        down = pltpu.roll(plane, 1, 0)
        down = self.put(0, self.got(0, i) * self.inside, down)
        return up - self.put(n - 1, self.got(1, i), down)


def matrix_x_kernel(
    field_ref, weight_ref, c_ref, rows_ref, token_ref,
    inv_ref, gam_ref, tau_ref, mat_ref, up_ref,
):
    n = c_ref.shape[0]
    rows = Rows(c_ref.shape[1:], rows_ref, not_first("gy"))
    up_ref[0] = rows.difference(field_ref, n - 1)
    weight = rows.plane(weight_ref, 2, n - 1) * 0.25
    before = rows.difference(field_ref, n - 2)
    up_ref[1] = rows.plane(field_ref, 0, n - 1) - weight * before
    up_ref[2] = weight
    left = STEP * rows.plane(c_ref, 3, 0)
    t = left
    a = jnp.zeros_like(t)
    ground = jnp.ones_like(t)
    for i in range(n - 1):
        c = STEP * rows.plane(c_ref, 3, i + 1)
        inv = 1.0 / (t + ground + c)
        gam = c * inv
        tau = t * inv
        inv_ref[i] = inv
        gam_ref[i] = gam
        tau_ref[i] = tau
        a = a + tau * ground
        ground = 1.0 + gam * ground
        t = t * gam
    up_ref[3] = ground + t * (1.0 - not_first("gx"))
    for k, value in enumerate((t, a, left)):
        mat_ref[k] = value


def forward_x_kernel(
    field_ref, weight_ref, rows_ref, inv_ref, gam_ref, tau_ref, phi_ref, side_ref,
):
    n = field_ref.shape[0]
    rows = Rows(field_ref.shape[1:], rows_ref, not_first("gy"))
    diffs = {-1: 0.0, 0: rows.difference(field_ref, 0)}
    side_ref[3] = diffs[0]
    q = j = 0.0
    for i in range(n - 1):
        diffs[i + 1] = rows.difference(field_ref, i + 1)
        weight = rows.plane(weight_ref, 2, i) * 0.25
        if i == 0:
            side_ref[2] = weight
        h = rows.plane(field_ref, 0, i) + weight * (diffs[i + 1] - diffs.pop(i - 1)) + q
        phi_ref[i] = inv_ref[i] * h
        q = gam_ref[i] * h
        j = j + tau_ref[i] * h
    side_ref[0] = j
    side_ref[1] = q


def finish_x_kernel(got_ref, mat_ref, side_ref, buf_ref, extra_ref):
    inside = not_first("gx")
    t, a, left = (mat_ref[k] for k in range(3))
    f0 = side_ref[2] * got_ref[0] * -inside
    extra = f0 / left
    source = got_ref[1] + got_ref[2] * side_ref[3] * inside
    j = (side_ref[0] + f0 - (a + t) * extra) * inside + source
    q = side_ref[1] + t * extra
    extra_ref[...] = extra
    store_values(buf_ref, [t * inside, got_ref[3] + a * inside, j, q])


def solve_kernel(n, m, halves, count, in_ref, out_ref):
    stride = m * count * halves

    def get(k):
        return jnp.concatenate(
            [
                in_ref[pl.ds((l * count + k) * halves + h, n, stride=stride), :]
                for l in range(m)
                for h in range(halves)
            ],
            axis=1,
        )

    def after(v, d=1):
        return pltpu.roll(v, n - d, 0)

    def before(v, d=1):
        return pltpu.roll(v, d, 0)

    low, g, j, q, *ground = (get(k) for k in range(count))
    g = after(g)
    if ground:
        g = g + ground[0]
    high = after(low)
    r = q + after(j)
    d = 1
    while d < n:
        inv = 1.0 / (g + low + high)
        gi = g * inv
        ri = r * inv
        g, r, low, high = (
            g + low * before(gi, d) + high * after(gi, d),
            r + low * before(ri, d) + high * after(ri, d),
            low * before(low * inv, d),
            high * after(high * inv, d),
        )
        d *= 2
    u = r / g
    u_prev = before(u)
    for l in range(m):
        for k, value in enumerate((u_prev, u)):
            for h in range(halves):
                at = (l * halves + h) * LANES
                out_ref[pl.ds((l * 2 + k) * halves + h, n, stride=m * 2 * halves), :] = value[
                    :, at : at + LANES
                ]


def backward(n, u_prev, u_own, gam_ref, tau_ref, phi_ref, emit):
    u = u_own
    emit(n - 1, u)
    for i in range(n - 2, -1, -1):
        u = (phi_ref[i] + tau_ref[i] * u_prev) + gam_ref[i] * u
        emit(i, u)


def middle_kernel(
    shape, ends_ref, extra_ref, phi_x_ref, gam_x_ref, tau_x_ref, c_ref,
    phi_ref, gam_ref, tau_ref, buf_ref, half_ref,
):
    nx, ny, nz = shape
    u_prev, u_own = load_values(ends_ref, ny, 2, nz // LANES)
    backward(nx, u_prev * not_first("gx") + extra_ref[...], u_own, gam_x_ref, tau_x_ref, phi_x_ref,
             lambda i, u: store_plane(half_ref, shape, i, u))
    t = STEP * load_y_whole(c_ref, shape, 0)
    a = jnp.zeros_like(t)
    ground = jnp.ones_like(t)
    q = j = 0.0
    for y in range(ny - 1):
        c = STEP * load_y_whole(c_ref, shape, y + 1)
        h = load_y(half_ref, shape, y) + q
        inv = 1.0 / (t + ground + c)
        gam = c * inv
        tau = t * inv
        phi_ref[y] = inv * h
        gam_ref[y] = gam
        tau_ref[y] = tau
        q = gam * h
        j = j + tau * h
        a = a + tau * ground
        ground = 1.0 + gam * ground
        t = t * gam
    inside = not_first("gy")
    j = j * inside + load_y(half_ref, shape, ny - 1)
    store_values(buf_ref, [t * inside, a * inside, j, q, ground + t * (1.0 - inside)])


def backward_y_kernel(shape, ends_ref, phi_ref, gam_ref, tau_ref, out_hbm, out_ref, sem):
    nx, ny, nz = shape
    u_prev, u_own = load_values(ends_ref, nx, 2, nz // LANES)
    copies = []

    def emit(y, u):
        store_y(out_ref, shape, y, u)
        if y % SUB == 0:
            copies.append(y_block_out(out_ref, out_hbm, y // SUB, sem))
            copies[-1].start()

    backward(ny, u_prev * not_first("gy"), u_own, gam_ref, tau_ref, phi_ref, emit)
    for copy in copies:
        copy.wait()


IN_VMEM = pl.BlockSpec(memory_space=pltpu.VMEM)
IN_PLACE = pl.BlockSpec(memory_space=pl.ANY)


def call(kernel, args, outs, name, scratch=(), hbm_args=(), hbm_outs=(), bytes_accessed=1 << 20,
         limit=16 * MIB):
    return pl.pallas_call(
        kernel,
        out_shape=[jax.ShapeDtypeStruct(s, f32) for s in outs],
        in_specs=[IN_PLACE if k in hbm_args else IN_VMEM for k in range(len(args))],
        out_specs=[IN_PLACE if k in hbm_outs else IN_VMEM for k in range(len(outs))],
        scratch_shapes=list(scratch),
        compiler_params=pltpu.CompilerParams(vmem_limit_bytes=limit),
        cost_estimate=pl.CostEstimate(flops=1 << 20, bytes_accessed=bytes_accessed, transcendentals=0),
        name=name,
    )(*args)


def from_before(value, axis):
    n = lax.axis_size(axis)
    return lax.ppermute(value, axis, [(i, (i + 1) % n) for i in range(n)])


def exchange(buf, axis):
    n = lax.axis_size(axis)
    rows, lanes = buf.shape
    got = lax.all_to_all(buf.reshape(n, 1, rows * lanes // n), axis, 0, 0, tiled=True)
    return got.reshape(rows, lanes)


def interfaces(buf, axis, lines, halves, count):
    n = lax.axis_size(axis)
    m = lines // n
    every = exchange(buf, axis)
    kernel = functools.partial(solve_kernel, n, m, halves, count)
    (ends,) = call(kernel, [every], [(n * m * 2 * halves, LANES)], "solve_" + axis)
    return exchange(ends, axis)


def shards(field, cond_x, cond_y, cross_weight):
    shape = nx, ny, nz = field.shape
    halves = nz // LANES
    x_plane = (ny, nz)
    y_plane = (nx, nz)
    blocks = pltpu.SemaphoreType.DMA((ny // SUB,))
    tile = pltpu.VMEM((nx, SUB, nz), f32)
    (rows,) = call(
        pack_kernel, [field, cross_weight, cond_x], [(4, *y_plane)], "pack",
        scratch=(tile, tile, tile, pltpu.SemaphoreType.DMA((3,))), hbm_args=(0, 1, 2),
        limit=MOST_VMEM,
    )
    rows = from_before(rows, "gy")
    (token,) = call(stage_kernel, [field, cross_weight, cond_x], [(SUB, LANES)], "stage")
    inv_x, gam_x, tau_x, mat_x, up = call(
        matrix_x_kernel, [field, cross_weight, cond_x, rows, token],
        [(nx - 1, *x_plane)] * 3 + [(3, *x_plane), (4, *x_plane)], "matrix_x",
    )
    got = from_before(up, "gx")
    phi_x, side = call(
        forward_x_kernel, [field, cross_weight, rows, inv_x, gam_x, tau_x],
        [(nx - 1, *x_plane), (4, *x_plane)], "forward_x", bytes_accessed=4 << 20,
    )
    buf_x, extra = call(
        finish_x_kernel, [got, mat_x, side], [(ny * 4 * halves, LANES), x_plane], "finish_x"
    )
    ends_x = interfaces(buf_x, "gx", ny, halves, 4)
    phi_y, gam_y, tau_y, buf_y = call(
        functools.partial(middle_kernel, shape),
        [ends_x, extra, phi_x, gam_x, tau_x, tile_rows(cond_y)],
        [(ny - 1, *y_plane)] * 3 + [(nx * 5 * halves, LANES)], "middle",
        scratch=(y_scratch(shape),),
    )
    ends_y = interfaces(buf_y, "gy", nx, halves, 5)
    (out,) = call(
        functools.partial(backward_y_kernel, shape), [ends_y, phi_y, gam_y, tau_y],
        [(nx, ny // SUB, SUB * halves, LANES)], "backward_y",
        scratch=(y_scratch(shape), blocks), hbm_outs=(0,),
    )
    return from_y_blocks(out, shape)


def solution(mesh):
    spec = P("gx", "gy", None)
    return jax.shard_map(
        shards, mesh=mesh, in_specs=(spec,) * 4, out_specs=spec, check_vma=False
    )
```

```python
import functools
import itertools

import jax
import jax.numpy as jnp
from jax import lax
from jax.experimental import pallas as pl
from jax.experimental.pallas import tpu as pltpu
from jax.sharding import PartitionSpec as P

STEP = 16384.0
LANES = 128
SUB = 8
MIB = 1 << 20
MOST_VMEM = 60817408
f32 = jnp.float32


def tile_rows(x):
    nx, ny, nz = x.shape
    x = x.reshape(nx, ny // SUB, SUB, nz // LANES, LANES)
    return x.transpose(0, 1, 3, 2, 4).reshape(nx * ny * nz // LANES, LANES)


def from_y_blocks(v, shape):
    nx, ny, nz = shape
    v = v.reshape(nx, ny // SUB, nz // LANES, SUB, LANES)
    return v.transpose(0, 1, 3, 2, 4).reshape(nx, ny, nz)


def y_scratch(shape):
    nx, ny, nz = shape
    return pltpu.VMEM((ny // SUB, nx * nz * SUB // LANES, LANES), f32)


def y_rows(shape, y, h):
    nx, _, nz = shape
    return y // SUB, pl.ds(h * SUB + y % SUB, nx, stride=SUB * nz // LANES), slice(None)


def load_y(ref, shape, y):
    return jnp.concatenate([ref[y_rows(shape, y, h)] for h in range(shape[2] // LANES)], axis=1)


def load_y_whole(ref, shape, y):
    nx, ny, nz = shape
    at = y // SUB * SUB * (nz // LANES) + y % SUB
    parts = [
        ref[pl.ds(at + h * SUB, nx, stride=ny * nz // LANES), :] for h in range(nz // LANES)
    ]
    return jnp.concatenate(parts, axis=1)


def store_y(ref, shape, y, value):
    for h in range(shape[2] // LANES):
        ref[y_rows(shape, y, h)] = value[:, h * LANES : (h + 1) * LANES]


def store_plane(ref, shape, x, value):
    _, ny, nz = shape
    halves = nz // LANES
    for yb in range(ny // SUB):
        for h in range(halves):
            start = (x * halves + h) * SUB
            ref[yb, start : start + SUB, :] = value[
                yb * SUB : (yb + 1) * SUB, h * LANES : (h + 1) * LANES
            ]


def y_block_out(scratch, hbm, yb, sem):
    block = scratch.at[yb].reshape(hbm.shape[0], hbm.shape[2], LANES)
    return pltpu.make_async_copy(block, hbm.at[:, yb], sem.at[yb])


def store_values(ref, values):
    lines, width = values[0].shape
    halves = width // LANES
    for k, value in enumerate(values):
        for h in range(halves):
            ref[pl.ds(k * halves + h, lines, stride=len(values) * halves), :] = value[
                :, h * LANES : (h + 1) * LANES
            ]


def load_values(ref, lines, count, halves):
    return [
        jnp.concatenate(
            [ref[pl.ds(k * halves + h, lines, stride=count * halves), :] for h in range(halves)],
            axis=1,
        )
        for k in range(count)
    ]


def pack_kernel(ny, field_hbm, weight_hbm, c_hbm, rows_ref, sem):
    nx, per_x = field_hbm.shape[0], field_hbm.shape[1]
    halves = per_x // ny
    copies = []
    for k, (hbm, y) in enumerate(
        ((field_hbm, ny - 1), (field_hbm, ny - 2), (weight_hbm, ny - 1), (c_hbm, ny - 1))
    ):
        for h in range(halves):
            at = (y // SUB * halves + h) * SUB + y % SUB
            place = k * halves + h
            copies.append(
                pltpu.make_async_copy(
                    hbm.at[:, at], rows_ref.at[pl.ds(place * nx, nx)], sem.at[place]
                )
            )
    for copy in copies:
        copy.start()
    for copy in copies:
        copy.wait()


def not_first(axis):
    return jnp.where(lax.axis_index(axis) == 0, 0.0, 1.0).astype(f32)


class Rows:
    def __init__(self, shape, rows_ref, inside):
        self.nx, self.n = shape[:2]
        self.row = lax.broadcasted_iota(jnp.int32, shape[1:], 0)
        self.rows_ref = rows_ref
        self.inside = inside

    def put(self, place, row, plane):
        return jnp.where(self.row == place, row, plane)

    def got(self, k, i):
        halves = self.row.shape[1] // LANES
        at = [(k * halves + h) * self.nx + i for h in range(halves)]
        return jnp.concatenate([self.rows_ref[r : r + 1, :] for r in at], axis=1)

    def plane(self, ref, k, i):
        return self.put(self.n - 1, self.got(k, i), ref[i])

    def difference(self, ref, i):
        n = self.n
        plane = ref[i]
        up = pltpu.roll(plane, n - 1, 0)
        up = self.put(n - 1, up * self.inside, up)
        down = pltpu.roll(plane, 1, 0)
        down = self.put(0, self.got(0, i) * self.inside, down)
        return up - self.put(n - 1, self.got(1, i), down)


def ahead_kernel(field_ref, weight_ref, c_ref, up_ref, corner_ref):
    n, ny, _ = c_ref.shape
    inside = not_first("gy")
    row = lax.broadcasted_iota(jnp.int32, c_ref.shape[1:], 0)
    edge = (row == 0) | (row == ny - 1)

    def difference(plane):
        up = pltpu.roll(plane, ny - 1, 0)
        up = jnp.where(row == ny - 1, up * inside, up)
        return up - jnp.where(edge, 0.0, pltpu.roll(plane, 1, 0))

    last, before = field_ref[n - 1], field_ref[n - 2]
    weight = weight_ref[n - 1] * 0.25
    before_difference = difference(before)
    up_ref[0] = difference(last)
    up_ref[1] = jnp.where(row == ny - 1, before_difference, last - weight * before_difference)
    up_ref[2] = weight
    t = STEP * c_ref[0]
    ground = jnp.ones_like(t)
    for i in range(n - 1):
        c = STEP * c_ref[i + 1]
        gam = c / (t + ground + c)
        ground = 1.0 + gam * ground
        t = t * gam
    ground = ground + t * (1.0 - not_first("gx"))
    up_ref[3] = ground
    for k, (plane, y) in enumerate(
        ((last, -1), (last, -2), (before, -1), (before, -2), (weight, -1), (ground, -1))
    ):
        corner_ref[k : k + 1, :] = plane[ny + y : ny + y + 1, :]
    corner_ref[6:8, :] = jnp.zeros_like(corner_ref[6:8, :])


def forward_x_kernel(
    field_ref, weight_ref, c_ref, rows_ref, up_ref, gam_ref, tau_ref, phi_ref, mat_ref, side_ref,
):
    n = c_ref.shape[0]
    rows = Rows(c_ref.shape, rows_ref, not_first("gy"))
    left = STEP * rows.plane(c_ref, 3, 0)
    t = left
    a = jnp.zeros_like(t)
    ground = jnp.ones_like(t)
    diffs = {-1: 0.0, 0: rows.difference(field_ref, 0)}
    side_ref[3] = diffs[0]
    q = j = 0.0
    for i in range(n - 1):
        c = STEP * rows.plane(c_ref, 3, i + 1)
        inv = 1.0 / (t + ground + c)
        gam = c * inv
        tau = t * inv
        gam_ref[i] = gam
        tau_ref[i] = tau
        a = a + tau * ground
        ground = 1.0 + gam * ground
        t = t * gam
        diffs[i + 1] = rows.difference(field_ref, i + 1)
        weight = rows.plane(weight_ref, 2, i) * 0.25
        if i == 0:
            side_ref[2] = weight
        h = rows.plane(field_ref, 0, i) + weight * (diffs[i + 1] - diffs.pop(i - 1)) + q
        phi_ref[i] = inv * h
        q = gam * h
        j = j + tau * h
    side_ref[0] = j
    side_ref[1] = q
    for k, value in enumerate((t, a, left)):
        mat_ref[k] = value


def finish_x_kernel(got_ref, corner_ref, mat_ref, side_ref, buf_ref, extra_ref):
    ny = got_ref.shape[1]
    inside_x, inside_y = not_first("gx"), not_first("gy")
    row = lax.broadcasted_iota(jnp.int32, got_ref.shape[1:], 0)
    first, last = row == 0, row == ny - 1
    f, f2, b, b2, w, ground = (corner_ref[k : k + 1, :] for k in range(6))
    difference = got_ref[0] - jnp.where(first, f * inside_y, jnp.where(last, f2, 0.0))
    weight = jnp.where(last, w, got_ref[2])
    partial = got_ref[1]
    partial = jnp.where(
        last,
        f - w * (partial - b2),
        partial + jnp.where(first, weight * (b * inside_y), 0.0),
    )
    grounds = jnp.where(last, ground, got_ref[3])
    t, a, left = (mat_ref[k] for k in range(3))
    f0 = side_ref[2] * difference * -inside_x
    extra = f0 / left
    source = partial + weight * side_ref[3] * inside_x
    j = (side_ref[0] + f0 - (a + t) * extra) * inside_x + source
    q = side_ref[1] + t * extra
    extra_ref[...] = extra
    store_values(buf_ref, [t * inside_x, grounds + a * inside_x, j, q])


def solve_kernel(n, m, halves, count, in_ref, out_ref):
    stride = m * count * halves

    def get(k):
        return jnp.concatenate(
            [
                in_ref[pl.ds((l * count + k) * halves + h, n, stride=stride), :]
                for l in range(m)
                for h in range(halves)
            ],
            axis=1,
        )

    def after(v, d=1):
        return pltpu.roll(v, n - d, 0)

    def before(v, d=1):
        return pltpu.roll(v, d, 0)

    low, g, j, q, *ground = (get(k) for k in range(count))
    g = after(g)
    if ground:
        g = g + ground[0]
    high = after(low)
    r = q + after(j)
    d = 1
    while d < n:
        inv = 1.0 / (g + low + high)
        gi = g * inv
        ri = r * inv
        g, r, low, high = (
            g + low * before(gi, d) + high * after(gi, d),
            r + low * before(ri, d) + high * after(ri, d),
            low * before(low * inv, d),
            high * after(high * inv, d),
        )
        d *= 2
    u = r / g
    u_prev = before(u)
    for l in range(m):
        for k, value in enumerate((u_prev, u)):
            for h in range(halves):
                at = (l * halves + h) * LANES
                out_ref[pl.ds((l * 2 + k) * halves + h, n, stride=m * 2 * halves), :] = value[
                    :, at : at + LANES
                ]


def backward(n, u_prev, u_own, gam_ref, tau_ref, phi_ref, emit):
    u = u_own
    emit(n - 1, u)
    for i in range(n - 2, -1, -1):
        u = (phi_ref[i] + tau_ref[i] * u_prev) + gam_ref[i] * u
        emit(i, u)


def middle_kernel(
    shape, ends_ref, extra_ref, phi_x_ref, gam_x_ref, tau_x_ref, c_ref,
    phi_ref, gam_ref, tau_ref, buf_ref, half_ref,
):
    nx, ny, nz = shape
    u_prev, u_own = load_values(ends_ref, ny, 2, nz // LANES)
    backward(nx, u_prev * not_first("gx") + extra_ref[...], u_own, gam_x_ref, tau_x_ref, phi_x_ref,
             lambda i, u: store_plane(half_ref, shape, i, u))
    t = STEP * load_y_whole(c_ref, shape, 0)
    a = jnp.zeros_like(t)
    ground = jnp.ones_like(t)
    q = j = 0.0
    for y in range(ny - 1):
        c = STEP * load_y_whole(c_ref, shape, y + 1)
        h = load_y(half_ref, shape, y) + q
        inv = 1.0 / (t + ground + c)
        gam = c * inv
        tau = t * inv
        phi_ref[y] = inv * h
        gam_ref[y] = gam
        tau_ref[y] = tau
        q = gam * h
        j = j + tau * h
        a = a + tau * ground
        ground = 1.0 + gam * ground
        t = t * gam
    inside = not_first("gy")
    j = j * inside + load_y(half_ref, shape, ny - 1)
    store_values(buf_ref, [t * inside, a * inside, j, q, ground + t * (1.0 - inside)])


def backward_y_kernel(shape, ends_ref, phi_ref, gam_ref, tau_ref, out_hbm, out_ref, sem):
    nx, ny, nz = shape
    u_prev, u_own = load_values(ends_ref, nx, 2, nz // LANES)
    copies = []

    def emit(y, u):
        store_y(out_ref, shape, y, u)
        if y % SUB == 0:
            copies.append(y_block_out(out_ref, out_hbm, y // SUB, sem))
            copies[-1].start()

    backward(ny, u_prev * not_first("gy"), u_own, gam_ref, tau_ref, phi_ref, emit)
    for copy in copies:
        copy.wait()


IN_VMEM = pl.BlockSpec(memory_space=pltpu.VMEM)
IN_PLACE = pl.BlockSpec(memory_space=pl.ANY)


def call(kernel, args, outs, name, scratch=(), hbm_args=(), hbm_outs=(), bytes_accessed=1 << 20,
         limit=16 * MIB):
    return pl.pallas_call(
        kernel,
        out_shape=[jax.ShapeDtypeStruct(s, f32) for s in outs],
        in_specs=[IN_PLACE if k in hbm_args else IN_VMEM for k in range(len(args))],
        out_specs=[IN_PLACE if k in hbm_outs else IN_VMEM for k in range(len(outs))],
        scratch_shapes=list(scratch),
        compiler_params=pltpu.CompilerParams(vmem_limit_bytes=limit),
        cost_estimate=pl.CostEstimate(flops=1 << 20, bytes_accessed=bytes_accessed, transcendentals=0),
        name=name,
    )(*args)


def from_before(value, *axes):
    sizes = [lax.axis_size(axis) for axis in axes]

    def index(place):
        at = 0
        for i, n in zip(place, sizes, strict=True):
            at = at * n + i % n
        return at

    places = itertools.product(*(range(n) for n in sizes))
    pairs = [(index(place), index([i + 1 for i in place])) for place in places]
    return lax.ppermute(value, axes, pairs)


def exchange(buf, axis):
    n = lax.axis_size(axis)
    rows, lanes = buf.shape
    got = lax.all_to_all(buf.reshape(n, 1, rows * lanes // n), axis, 0, 0, tiled=True)
    return got.reshape(rows, lanes)


def interfaces(buf, axis, lines, halves, count):
    n = lax.axis_size(axis)
    m = lines // n
    every = exchange(buf, axis)
    kernel = functools.partial(solve_kernel, n, m, halves, count)
    (ends,) = call(kernel, [every], [(n * m * 2 * halves, LANES)], "solve_" + axis)
    return exchange(ends, axis)


def shards(field, cond_x, cond_y, cross_weight):
    shape = nx, ny, nz = field.shape
    halves = nz // LANES
    x_plane = (ny, nz)
    y_plane = (nx, nz)
    blocks = pltpu.SemaphoreType.DMA((ny // SUB,))
    single = [tile_rows(v).reshape(nx, ny * halves, 1, LANES) for v in (field, cross_weight, cond_x)]
    (rows,) = call(
        functools.partial(pack_kernel, ny), single, [(4 * halves * nx, 1, LANES)], "pack",
        scratch=(pltpu.SemaphoreType.DMA((4 * halves,)),), hbm_args=(0, 1, 2), limit=MOST_VMEM,
    )
    rows = from_before(rows, "gy").reshape(4 * halves * nx, LANES)
    up, corner = call(
        ahead_kernel, [field, cross_weight, cond_x], [(4, *x_plane), (SUB, nz)], "ahead"
    )
    corner = from_before(corner, "gx", "gy")
    got = from_before(up, "gx")
    gam_x, tau_x, phi_x, mat_x, side = call(
        forward_x_kernel, [field, cross_weight, cond_x, rows, up],
        [(nx - 1, *x_plane)] * 3 + [(3, *x_plane), (4, *x_plane)], "forward_x",
    )
    buf_x, extra = call(
        finish_x_kernel, [got, corner, mat_x, side], [(ny * 4 * halves, LANES), x_plane], "finish_x"
    )
    ends_x = interfaces(buf_x, "gx", ny, halves, 4)
    phi_y, gam_y, tau_y, buf_y = call(
        functools.partial(middle_kernel, shape),
        [ends_x, extra, phi_x, gam_x, tau_x, tile_rows(cond_y)],
        [(ny - 1, *y_plane)] * 3 + [(nx * 5 * halves, LANES)], "middle",
        scratch=(y_scratch(shape),),
    )
    ends_y = interfaces(buf_y, "gy", nx, halves, 5)
    (out,) = call(
        functools.partial(backward_y_kernel, shape), [ends_y, phi_y, gam_y, tau_y],
        [(nx, ny // SUB, SUB * halves, LANES)], "backward_y",
        scratch=(y_scratch(shape), blocks), hbm_outs=(0,),
    )
    return from_y_blocks(out, shape)


def solution(mesh):
    spec = P("gx", "gy", None)
    return jax.shard_map(
        shards, mesh=mesh, in_specs=(spec,) * 4, out_specs=spec, check_vma=False
    )
```

```python
import functools
import itertools

import jax
import jax.numpy as jnp
from jax import lax
from jax.experimental import pallas as pl
from jax.experimental.pallas import tpu as pltpu
from jax.sharding import PartitionSpec as P

STEP = 16384.0
LANES = 128
SUB = 8
MIB = 1 << 20
MOST_VMEM = 55574528
f32 = jnp.float32


def tile_rows(x):
    nx, ny, nz = x.shape
    x = x.reshape(nx, ny // SUB, SUB, nz // LANES, LANES)
    return x.transpose(0, 1, 3, 2, 4).reshape(nx * ny * nz // LANES, LANES)


def from_y_blocks(v, shape):
    nx, ny, nz = shape
    v = v.reshape(nx, ny // SUB, nz // LANES, SUB, LANES)
    return v.transpose(0, 1, 3, 2, 4).reshape(nx, ny, nz)


def y_scratch(shape):
    nx, ny, nz = shape
    return pltpu.VMEM((ny // SUB, nx * nz * SUB // LANES, LANES), f32)


def y_rows(shape, y, h):
    nx, _, nz = shape
    return y // SUB, pl.ds(h * SUB + y % SUB, nx, stride=SUB * nz // LANES), slice(None)


def load_y(ref, shape, y):
    return jnp.concatenate([ref[y_rows(shape, y, h)] for h in range(shape[2] // LANES)], axis=1)


def load_y_whole(ref, shape, y):
    nx, ny, nz = shape
    at = y // SUB * SUB * (nz // LANES) + y % SUB
    parts = [
        ref[pl.ds(at + h * SUB, nx, stride=ny * nz // LANES), :] for h in range(nz // LANES)
    ]
    return jnp.concatenate(parts, axis=1)


def store_y(ref, shape, y, value):
    for h in range(shape[2] // LANES):
        ref[y_rows(shape, y, h)] = value[:, h * LANES : (h + 1) * LANES]


def store_plane(ref, shape, x, value):
    _, ny, nz = shape
    halves = nz // LANES
    for yb in range(ny // SUB):
        for h in range(halves):
            start = (x * halves + h) * SUB
            ref[yb, start : start + SUB, :] = value[
                yb * SUB : (yb + 1) * SUB, h * LANES : (h + 1) * LANES
            ]


def y_block_out(scratch, hbm, yb, sem):
    block = scratch.at[yb].reshape(hbm.shape[0], hbm.shape[2], LANES)
    return pltpu.make_async_copy(block, hbm.at[:, yb], sem.at[yb])


def store_values(ref, values):
    lines, width = values[0].shape
    halves = width // LANES
    for k, value in enumerate(values):
        for h in range(halves):
            ref[pl.ds(k * halves + h, lines, stride=len(values) * halves), :] = value[
                :, h * LANES : (h + 1) * LANES
            ]


def load_values(ref, lines, count, halves):
    return [
        jnp.concatenate(
            [ref[pl.ds(k * halves + h, lines, stride=count * halves), :] for h in range(halves)],
            axis=1,
        )
        for k in range(count)
    ]


def pack_kernel(ny, field_hbm, weight_hbm, c_hbm, rows_ref, sem):
    nx, per_x = field_hbm.shape[0], field_hbm.shape[1]
    halves = per_x // ny
    copies = []
    for k, (hbm, y) in enumerate(
        ((field_hbm, ny - 1), (field_hbm, ny - 2), (weight_hbm, ny - 1), (c_hbm, ny - 1))
    ):
        for h in range(halves):
            at = (y // SUB * halves + h) * SUB + y % SUB
            place = k * halves + h
            copies.append(
                pltpu.make_async_copy(
                    hbm.at[:, at], rows_ref.at[pl.ds(place * nx, nx)], sem.at[place]
                )
            )
    for copy in copies:
        copy.start()
    for copy in copies:
        copy.wait()


def not_first(axis):
    return jnp.where(lax.axis_index(axis) == 0, 0.0, 1.0).astype(f32)


class Rows:
    def __init__(self, shape, rows_ref, inside):
        self.nx, self.n = shape[:2]
        self.row = lax.broadcasted_iota(jnp.int32, shape[1:], 0)
        self.rows_ref = rows_ref
        self.inside = inside

    def put(self, place, row, plane):
        return jnp.where(self.row == place, row, plane)

    def got(self, k, i):
        halves = self.row.shape[1] // LANES
        at = [(k * halves + h) * self.nx + i for h in range(halves)]
        return jnp.concatenate([self.rows_ref[r : r + 1, :] for r in at], axis=1)

    def plane(self, ref, k, i):
        return self.put(self.n - 1, self.got(k, i), ref[i])

    def difference(self, ref, i):
        n = self.n
        plane = ref[i]
        up = pltpu.roll(plane, n - 1, 0)
        up = self.put(n - 1, up * self.inside, up)
        down = pltpu.roll(plane, 1, 0)
        down = self.put(0, self.got(0, i) * self.inside, down)
        return up - self.put(n - 1, self.got(1, i), down)


def ahead_kernel(field_ref, weight_ref, c_ref, up_ref, corner_ref):
    n, ny, _ = c_ref.shape
    inside = not_first("gy")
    row = lax.broadcasted_iota(jnp.int32, c_ref.shape[1:], 0)
    edge = (row == 0) | (row == ny - 1)

    def difference(plane):
        up = pltpu.roll(plane, ny - 1, 0)
        up = jnp.where(row == ny - 1, up * inside, up)
        return up - jnp.where(edge, 0.0, pltpu.roll(plane, 1, 0))

    last, before = field_ref[n - 1], field_ref[n - 2]
    weight = weight_ref[n - 1] * 0.25
    before_difference = difference(before)
    up_ref[0] = difference(last)
    up_ref[1] = jnp.where(row == ny - 1, before_difference, last - weight * before_difference)
    up_ref[2] = weight
    t = STEP * c_ref[0]
    ground = jnp.ones_like(t)
    for i in range(n - 1):
        c = STEP * c_ref[i + 1]
        gam = c / (t + ground + c)
        ground = 1.0 + gam * ground
        t = t * gam
    ground = ground + t * (1.0 - not_first("gx"))
    up_ref[3] = ground
    for k, (plane, y) in enumerate(
        ((last, -1), (last, -2), (before, -1), (before, -2), (weight, -1), (ground, -1))
    ):
        corner_ref[k : k + 1, :] = plane[ny + y : ny + y + 1, :]
    corner_ref[6:8, :] = jnp.zeros_like(corner_ref[6:8, :])


def forward_x_kernel(
    field_ref, weight_ref, c_ref, rows_ref, up_ref, gam_ref, tau_ref, phi_ref, mat_ref, side_ref,
):
    n = c_ref.shape[0]
    rows = Rows(c_ref.shape, rows_ref, not_first("gy"))
    left = STEP * rows.plane(c_ref, 3, 0)
    t = left
    a = jnp.zeros_like(t)
    ground = jnp.ones_like(t)
    diffs = {-1: 0.0, 0: rows.difference(field_ref, 0)}
    side_ref[3] = diffs[0]
    q = j = 0.0
    for i in range(n - 1):
        c = STEP * rows.plane(c_ref, 3, i + 1)
        inv = 1.0 / (t + ground + c)
        gam = c * inv
        tau = t * inv
        gam_ref[i] = gam
        tau_ref[i] = tau
        a = a + tau * ground
        ground = 1.0 + gam * ground
        t = t * gam
        diffs[i + 1] = rows.difference(field_ref, i + 1)
        weight = rows.plane(weight_ref, 2, i) * 0.25
        if i == 0:
            side_ref[2] = weight
        h = rows.plane(field_ref, 0, i) + weight * (diffs[i + 1] - diffs.pop(i - 1)) + q
        phi_ref[i] = inv * h
        q = gam * h
        j = j + tau * h
    side_ref[0] = j
    side_ref[1] = q
    for k, value in enumerate((t, a, left)):
        mat_ref[k] = value


def finish_x_kernel(got_ref, corner_ref, mat_ref, side_ref, buf_ref, extra_ref):
    ny = got_ref.shape[1]
    inside_x, inside_y = not_first("gx"), not_first("gy")
    row = lax.broadcasted_iota(jnp.int32, got_ref.shape[1:], 0)
    first, last = row == 0, row == ny - 1
    f, f2, b, b2, w, ground = (corner_ref[k : k + 1, :] for k in range(6))
    difference = got_ref[0] - jnp.where(first, f * inside_y, jnp.where(last, f2, 0.0))
    weight = jnp.where(last, w, got_ref[2])
    partial = got_ref[1]
    partial = jnp.where(
        last,
        f - w * (partial - b2),
        partial + jnp.where(first, weight * (b * inside_y), 0.0),
    )
    grounds = jnp.where(last, ground, got_ref[3])
    t, a, left = (mat_ref[k] for k in range(3))
    f0 = side_ref[2] * difference * -inside_x
    extra = f0 / left
    source = partial + weight * side_ref[3] * inside_x
    j = (side_ref[0] + f0 - (a + t) * extra) * inside_x + source
    q = side_ref[1] + t * extra
    extra_ref[...] = extra
    store_values(buf_ref, [t * inside_x, grounds + a * inside_x, j, q])


def solve_kernel(n, m, halves, count, in_ref, out_ref):
    stride = m * count * halves

    def get(k):
        return jnp.concatenate(
            [
                in_ref[pl.ds((l * count + k) * halves + h, n, stride=stride), :]
                for l in range(m)
                for h in range(halves)
            ],
            axis=1,
        )

    def after(v, d=1):
        return pltpu.roll(v, n - d, 0)

    def before(v, d=1):
        return pltpu.roll(v, d, 0)

    low, g, j, q, *ground = (get(k) for k in range(count))
    g = after(g)
    if ground:
        g = g + ground[0]
    high = after(low)
    r = q + after(j)
    d = 1
    while d < n:
        inv = 1.0 / (g + low + high)
        gi = g * inv
        ri = r * inv
        g, r, low, high = (
            g + low * before(gi, d) + high * after(gi, d),
            r + low * before(ri, d) + high * after(ri, d),
            low * before(low * inv, d),
            high * after(high * inv, d),
        )
        d *= 2
    u = r / g
    u_prev = before(u)
    for l in range(m):
        for k, value in enumerate((u_prev, u)):
            for h in range(halves):
                at = (l * halves + h) * LANES
                out_ref[pl.ds((l * 2 + k) * halves + h, n, stride=m * 2 * halves), :] = value[
                    :, at : at + LANES
                ]


def backward(n, u_prev, u_own, gam_ref, tau_ref, phi_ref, emit):
    u = u_own
    emit(n - 1, u)
    for i in range(n - 2, -1, -1):
        u = (phi_ref[i] + tau_ref[i] * u_prev) + gam_ref[i] * u
        emit(i, u)


def middle_kernel(
    shape, ends_ref, extra_ref, phi_x_ref, gam_x_ref, tau_x_ref, c_ref,
    phi_ref, gam_ref, tau_ref, buf_ref, half_ref,
):
    nx, ny, nz = shape
    u_prev, u_own = load_values(ends_ref, ny, 2, nz // LANES)
    backward(nx, u_prev * not_first("gx") + extra_ref[...], u_own, gam_x_ref, tau_x_ref, phi_x_ref,
             lambda i, u: store_plane(half_ref, shape, i, u))
    t = STEP * load_y_whole(c_ref, shape, 0)
    a = jnp.zeros_like(t)
    ground = jnp.ones_like(t)
    q = j = 0.0
    for y in range(ny - 1):
        c = STEP * load_y_whole(c_ref, shape, y + 1)
        h = load_y(half_ref, shape, y) + q
        inv = 1.0 / (t + ground + c)
        gam = c * inv
        tau = t * inv
        phi_ref[y] = inv * h
        gam_ref[y] = gam
        tau_ref[y] = tau
        q = gam * h
        j = j + tau * h
        a = a + tau * ground
        ground = 1.0 + gam * ground
        t = t * gam
    inside = not_first("gy")
    j = j * inside + load_y(half_ref, shape, ny - 1)
    store_values(buf_ref, [t * inside, a * inside, j, q, ground + t * (1.0 - inside)])


def backward_y_kernel(shape, ends_ref, phi_ref, gam_ref, tau_ref, out_hbm, out_ref, sem):
    nx, ny, nz = shape
    u_prev, u_own = load_values(ends_ref, nx, 2, nz // LANES)
    copies = []

    def emit(y, u):
        store_y(out_ref, shape, y, u)
        if y % SUB == 0:
            copies.append(y_block_out(out_ref, out_hbm, y // SUB, sem))
            copies[-1].start()

    backward(ny, u_prev * not_first("gy"), u_own, gam_ref, tau_ref, phi_ref, emit)
    for copy in copies:
        copy.wait()


IN_VMEM = pl.BlockSpec(memory_space=pltpu.VMEM)
IN_PLACE = pl.BlockSpec(memory_space=pl.ANY)


def call(kernel, args, outs, name, scratch=(), hbm_args=(), hbm_outs=(), bytes_accessed=1 << 20,
         limit=16 * MIB):
    return pl.pallas_call(
        kernel,
        out_shape=[jax.ShapeDtypeStruct(s, f32) for s in outs],
        in_specs=[IN_PLACE if k in hbm_args else IN_VMEM for k in range(len(args))],
        out_specs=[IN_PLACE if k in hbm_outs else IN_VMEM for k in range(len(outs))],
        scratch_shapes=list(scratch),
        compiler_params=pltpu.CompilerParams(vmem_limit_bytes=limit),
        cost_estimate=pl.CostEstimate(flops=1 << 20, bytes_accessed=bytes_accessed, transcendentals=0),
        name=name,
    )(*args)


def from_before(value, *axes):
    sizes = [lax.axis_size(axis) for axis in axes]

    def index(place):
        at = 0
        for i, n in zip(place, sizes, strict=True):
            at = at * n + i % n
        return at

    places = itertools.product(*(range(n) for n in sizes))
    pairs = [(index(place), index([i + 1 for i in place])) for place in places]
    return lax.ppermute(value, axes, pairs)


def exchange(buf, axis):
    n = lax.axis_size(axis)
    rows, lanes = buf.shape
    got = lax.all_to_all(buf.reshape(n, 1, rows * lanes // n), axis, 0, 0, tiled=True)
    return got.reshape(rows, lanes)


def interfaces(buf, axis, lines, halves, count):
    n = lax.axis_size(axis)
    m = lines // n
    every = exchange(buf, axis)
    kernel = functools.partial(solve_kernel, n, m, halves, count)
    (ends,) = call(kernel, [every], [(n * m * 2 * halves, LANES)], "solve_" + axis)
    return exchange(ends, axis)


def shards(field, cond_x, cond_y, cross_weight):
    shape = nx, ny, nz = field.shape
    halves = nz // LANES
    x_plane = (ny, nz)
    y_plane = (nx, nz)
    blocks = pltpu.SemaphoreType.DMA((ny // SUB,))
    single = [tile_rows(v).reshape(nx, ny * halves, 1, LANES) for v in (field, cross_weight, cond_x)]
    (rows,) = call(
        functools.partial(pack_kernel, ny), single, [(4 * halves * nx, 1, LANES)], "pack",
        scratch=(pltpu.SemaphoreType.DMA((4 * halves,)),), hbm_args=(0, 1, 2), limit=MOST_VMEM,
    )
    rows = from_before(rows, "gy").reshape(4 * halves * nx, LANES)
    up, corner = call(
        ahead_kernel, [field, cross_weight, cond_x], [(4, *x_plane), (SUB, nz)], "ahead"
    )
    corner = from_before(corner, "gx", "gy")
    got = from_before(up, "gx")
    gam_x, tau_x, phi_x, mat_x, side = call(
        forward_x_kernel, [field, cross_weight, cond_x, rows, up],
        [(nx - 1, *x_plane)] * 3 + [(3, *x_plane), (4, *x_plane)], "forward_x",
    )
    buf_x, extra = call(
        finish_x_kernel, [got, corner, mat_x, side], [(ny * 4 * halves, LANES), x_plane], "finish_x"
    )
    ends_x = interfaces(buf_x, "gx", ny, halves, 4)
    phi_y, gam_y, tau_y, buf_y = call(
        functools.partial(middle_kernel, shape),
        [ends_x, extra, phi_x, gam_x, tau_x, tile_rows(cond_y)],
        [(ny - 1, *y_plane)] * 3 + [(nx * 5 * halves, LANES)], "middle",
        scratch=(y_scratch(shape),),
    )
    ends_y = interfaces(buf_y, "gy", nx, halves, 5)
    (out,) = call(
        functools.partial(backward_y_kernel, shape), [ends_y, phi_y, gam_y, tau_y],
        [(nx, ny // SUB, SUB * halves, LANES)], "backward_y",
        scratch=(y_scratch(shape), blocks), hbm_outs=(0,),
    )
    return from_y_blocks(out, shape)


def solution(mesh):
    spec = P("gx", "gy", None)
    return jax.shard_map(
        shards, mesh=mesh, in_specs=(spec,) * 4, out_specs=spec, check_vma=False
    )
```

```python
import functools
import itertools

import jax
import jax.numpy as jnp
from jax import lax
from jax.experimental import pallas as pl
from jax.experimental.pallas import tpu as pltpu
from jax.sharding import PartitionSpec as P

STEP = 16384.0
LANES = 128
SPARE = 8
SUB = 8
MIB = 1 << 20
MOST_VMEM = 55574528
f32 = jnp.float32


def tile_rows(x):
    nx, ny, nz = x.shape
    x = x.reshape(nx, ny // SUB, SUB, nz // LANES, LANES)
    return x.transpose(0, 1, 3, 2, 4).reshape(nx * ny * nz // LANES, LANES)


def from_y_blocks(v, shape):
    nx, ny, nz = shape
    v = v.reshape(nx, ny // SUB, nz // LANES, SUB, LANES)
    return v.transpose(0, 1, 3, 2, 4).reshape(nx, ny, nz)


def y_scratch(shape):
    nx, ny, nz = shape
    return pltpu.VMEM((ny // SUB, nx * (nz * SUB // LANES + SPARE), LANES), f32)


def y_rows(shape, y, h):
    nx, _, nz = shape
    return y // SUB, pl.ds(h * SUB + y % SUB, nx, stride=SUB * nz // LANES + SPARE), slice(None)


def load_y(ref, shape, y):
    return jnp.concatenate([ref[y_rows(shape, y, h)] for h in range(shape[2] // LANES)], axis=1)


def load_y_whole(ref, shape, y):
    nx, ny, nz = shape
    at = y // SUB * SUB * (nz // LANES) + y % SUB
    parts = [
        ref[pl.ds(at + h * SUB, nx, stride=ny * nz // LANES), :] for h in range(nz // LANES)
    ]
    return jnp.concatenate(parts, axis=1)


def store_y(ref, shape, y, value):
    for h in range(shape[2] // LANES):
        ref[y_rows(shape, y, h)] = value[:, h * LANES : (h + 1) * LANES]


def store_plane(ref, shape, x, value):
    _, ny, nz = shape
    halves = nz // LANES
    for yb in range(ny // SUB):
        for h in range(halves):
            start = x * (halves * SUB + SPARE) + h * SUB
            ref[yb, start : start + SUB, :] = value[
                yb * SUB : (yb + 1) * SUB, h * LANES : (h + 1) * LANES
            ]


def y_block_out(scratch, hbm, yb, sem):
    rows = hbm.shape[2]
    block = scratch.at[yb].reshape(hbm.shape[0], rows + SPARE, LANES).at[:, pl.ds(0, rows)]
    return pltpu.make_async_copy(block, hbm.at[:, yb], sem.at[yb])


def store_values(ref, values):
    lines, width = values[0].shape
    halves = width // LANES
    for k, value in enumerate(values):
        for h in range(halves):
            ref[pl.ds(k * halves + h, lines, stride=len(values) * halves), :] = value[
                :, h * LANES : (h + 1) * LANES
            ]


def load_values(ref, lines, count, halves):
    return [
        jnp.concatenate(
            [ref[pl.ds(k * halves + h, lines, stride=count * halves), :] for h in range(halves)],
            axis=1,
        )
        for k in range(count)
    ]


def pack_kernel(ny, field_hbm, weight_hbm, c_hbm, rows_ref, sem):
    nx, per_x = field_hbm.shape[0], field_hbm.shape[1]
    halves = per_x // ny
    copies = []
    for k, (hbm, y) in enumerate(
        ((field_hbm, ny - 1), (field_hbm, ny - 2), (weight_hbm, ny - 1), (c_hbm, ny - 1))
    ):
        for h in range(halves):
            at = (y // SUB * halves + h) * SUB + y % SUB
            place = k * halves + h
            copies.append(
                pltpu.make_async_copy(
                    hbm.at[:, at], rows_ref.at[pl.ds(place * nx, nx)], sem.at[place]
                )
            )
    for copy in copies:
        copy.start()
    for copy in copies:
        copy.wait()


def not_first(axis):
    return jnp.where(lax.axis_index(axis) == 0, 0.0, 1.0).astype(f32)


class Rows:
    def __init__(self, shape, rows_ref, inside):
        self.nx, self.n = shape[:2]
        self.row = lax.broadcasted_iota(jnp.int32, shape[1:], 0)
        self.rows_ref = rows_ref
        self.inside = inside

    def put(self, place, row, plane):
        return jnp.where(self.row == place, row, plane)

    def got(self, k, i):
        halves = self.row.shape[1] // LANES
        at = [(k * halves + h) * self.nx + i for h in range(halves)]
        return jnp.concatenate([self.rows_ref[r : r + 1, :] for r in at], axis=1)

    def plane(self, ref, k, i):
        return self.put(self.n - 1, self.got(k, i), ref[i])

    def difference(self, ref, i):
        n = self.n
        plane = ref[i]
        up = pltpu.roll(plane, n - 1, 0)
        up = self.put(n - 1, up * self.inside, up)
        down = pltpu.roll(plane, 1, 0)
        down = self.put(0, self.got(0, i) * self.inside, down)
        return up - self.put(n - 1, self.got(1, i), down)


def ahead_kernel(field_ref, weight_ref, c_ref, up_ref, corner_ref):
    n, ny, _ = c_ref.shape
    inside = not_first("gy")
    row = lax.broadcasted_iota(jnp.int32, c_ref.shape[1:], 0)
    edge = (row == 0) | (row == ny - 1)

    def difference(plane):
        up = pltpu.roll(plane, ny - 1, 0)
        up = jnp.where(row == ny - 1, up * inside, up)
        return up - jnp.where(edge, 0.0, pltpu.roll(plane, 1, 0))

    last, before = field_ref[n - 1], field_ref[n - 2]
    weight = weight_ref[n - 1] * 0.25
    before_difference = difference(before)
    up_ref[0] = difference(last)
    up_ref[1] = jnp.where(row == ny - 1, before_difference, last - weight * before_difference)
    up_ref[2] = weight
    t = STEP * c_ref[0]
    ground = jnp.ones_like(t)
    for i in range(n - 1):
        c = STEP * c_ref[i + 1]
        gam = c / (t + ground + c)
        ground = 1.0 + gam * ground
        t = t * gam
    ground = ground + t * (1.0 - not_first("gx"))
    up_ref[3] = ground
    for k, (plane, y) in enumerate(
        ((last, -1), (last, -2), (before, -1), (before, -2), (weight, -1), (ground, -1))
    ):
        corner_ref[k : k + 1, :] = plane[ny + y : ny + y + 1, :]
    corner_ref[6:8, :] = jnp.zeros_like(corner_ref[6:8, :])


def forward_x_kernel(
    field_ref, weight_ref, c_ref, rows_ref, up_ref, gam_ref, tau_ref, phi_ref, mat_ref, side_ref,
):
    n = c_ref.shape[0]
    rows = Rows(c_ref.shape, rows_ref, not_first("gy"))
    left = STEP * rows.plane(c_ref, 3, 0)
    t = left
    a = jnp.zeros_like(t)
    ground = jnp.ones_like(t)
    diffs = {-1: 0.0, 0: rows.difference(field_ref, 0)}
    side_ref[3] = diffs[0]
    q = j = 0.0
    for i in range(n - 1):
        c = STEP * rows.plane(c_ref, 3, i + 1)
        inv = 1.0 / (t + ground + c)
        gam = c * inv
        tau = t * inv
        gam_ref[i] = gam
        tau_ref[i] = tau
        a = a + tau * ground
        ground = 1.0 + gam * ground
        t = t * gam
        diffs[i + 1] = rows.difference(field_ref, i + 1)
        weight = rows.plane(weight_ref, 2, i) * 0.25
        if i == 0:
            side_ref[2] = weight
        h = rows.plane(field_ref, 0, i) + weight * (diffs[i + 1] - diffs.pop(i - 1)) + q
        phi_ref[i] = inv * h
        q = gam * h
        j = j + tau * h
    side_ref[0] = j
    side_ref[1] = q
    for k, value in enumerate((t, a, left)):
        mat_ref[k] = value


def finish_x_kernel(got_ref, corner_ref, mat_ref, side_ref, turned_ref, buf_ref, extra_ref):
    ny = got_ref.shape[1]
    inside_x, inside_y = not_first("gx"), not_first("gy")
    row = lax.broadcasted_iota(jnp.int32, got_ref.shape[1:], 0)
    first, last = row == 0, row == ny - 1
    f, f2, b, b2, w, ground = (corner_ref[k : k + 1, :] for k in range(6))
    difference = got_ref[0] - jnp.where(first, f * inside_y, jnp.where(last, f2, 0.0))
    weight = jnp.where(last, w, got_ref[2])
    partial = got_ref[1]
    partial = jnp.where(
        last,
        f - w * (partial - b2),
        partial + jnp.where(first, weight * (b * inside_y), 0.0),
    )
    grounds = jnp.where(last, ground, got_ref[3])
    t, a, left = (mat_ref[k] for k in range(3))
    f0 = side_ref[2] * difference * -inside_x
    extra = f0 / left
    source = partial + weight * side_ref[3] * inside_x
    j = (side_ref[0] + f0 - (a + t) * extra) * inside_x + source
    q = side_ref[1] + t * extra
    extra_ref[...] = extra
    store_values(buf_ref, [t * inside_x, grounds + a * inside_x, j, q])


def solve_kernel(n, m, halves, count, in_ref, out_ref):
    stride = m * count * halves

    def get(k):
        return jnp.concatenate(
            [
                in_ref[pl.ds((l * count + k) * halves + h, n, stride=stride), :]
                for l in range(m)
                for h in range(halves)
            ],
            axis=1,
        )

    def after(v, d=1):
        return pltpu.roll(v, n - d, 0)

    def before(v, d=1):
        return pltpu.roll(v, d, 0)

    low, g, j, q, *ground = (get(k) for k in range(count))
    g = after(g)
    if ground:
        g = g + ground[0]
    high = after(low)
    r = q + after(j)
    d = 1
    while d < n:
        inv = 1.0 / (g + low + high)
        gi = g * inv
        ri = r * inv
        g, r, low, high = (
            g + low * before(gi, d) + high * after(gi, d),
            r + low * before(ri, d) + high * after(ri, d),
            low * before(low * inv, d),
            high * after(high * inv, d),
        )
        d *= 2
    u = r / g
    u_prev = before(u)
    for l in range(m):
        for k, value in enumerate((u_prev, u)):
            for h in range(halves):
                at = (l * halves + h) * LANES
                out_ref[pl.ds((l * 2 + k) * halves + h, n, stride=m * 2 * halves), :] = value[
                    :, at : at + LANES
                ]


def backward(n, u_prev, u_own, gam_ref, tau_ref, phi_ref, emit):
    u = u_own
    emit(n - 1, u)
    for i in range(n - 2, -1, -1):
        u = (phi_ref[i] + tau_ref[i] * u_prev) + gam_ref[i] * u
        emit(i, u)


def turn_kernel(shape, c_ref, out_ref):
    for y in range(shape[1]):
        out_ref[y] = STEP * load_y_whole(c_ref, shape, y)


def middle_kernel(
    shape, ends_ref, extra_ref, phi_x_ref, gam_x_ref, tau_x_ref, c_ref,
    phi_ref, gam_ref, tau_ref, buf_ref, half_ref,
):
    nx, ny, nz = shape
    u_prev, u_own = load_values(ends_ref, ny, 2, nz // LANES)
    backward(nx, u_prev * not_first("gx") + extra_ref[...], u_own, gam_x_ref, tau_x_ref, phi_x_ref,
             lambda i, u: store_plane(half_ref, shape, i, u))
    t = c_ref[0]
    a = jnp.zeros_like(t)
    ground = jnp.ones_like(t)
    q = j = 0.0
    for y in range(ny - 1):
        c = c_ref[y + 1]
        h = load_y(half_ref, shape, y) + q
        inv = 1.0 / (t + ground + c)
        gam = c * inv
        tau = t * inv
        phi_ref[y] = inv * h
        gam_ref[y] = gam
        tau_ref[y] = tau
        q = gam * h
        j = j + tau * h
        a = a + tau * ground
        ground = 1.0 + gam * ground
        t = t * gam
    inside = not_first("gy")
    j = j * inside + load_y(half_ref, shape, ny - 1)
    store_values(buf_ref, [t * inside, a * inside, j, q, ground + t * (1.0 - inside)])


def backward_y_kernel(shape, ends_ref, phi_ref, gam_ref, tau_ref, out_hbm, out_ref, sem):
    nx, ny, nz = shape
    u_prev, u_own = load_values(ends_ref, nx, 2, nz // LANES)
    copies = []

    def emit(y, u):
        store_y(out_ref, shape, y, u)
        if y % SUB == 0:
            copies.append(y_block_out(out_ref, out_hbm, y // SUB, sem))
            copies[-1].start()

    backward(ny, u_prev * not_first("gy"), u_own, gam_ref, tau_ref, phi_ref, emit)
    for copy in copies:
        copy.wait()


IN_VMEM = pl.BlockSpec(memory_space=pltpu.VMEM)
IN_PLACE = pl.BlockSpec(memory_space=pl.ANY)


def call(kernel, args, outs, name, scratch=(), hbm_args=(), hbm_outs=(), bytes_accessed=1 << 20,
         limit=16 * MIB):
    return pl.pallas_call(
        kernel,
        out_shape=[jax.ShapeDtypeStruct(s, f32) for s in outs],
        in_specs=[IN_PLACE if k in hbm_args else IN_VMEM for k in range(len(args))],
        out_specs=[IN_PLACE if k in hbm_outs else IN_VMEM for k in range(len(outs))],
        scratch_shapes=list(scratch),
        compiler_params=pltpu.CompilerParams(vmem_limit_bytes=limit),
        cost_estimate=pl.CostEstimate(flops=1 << 20, bytes_accessed=bytes_accessed, transcendentals=0),
        name=name,
    )(*args)


def from_before(value, *axes):
    sizes = [lax.axis_size(axis) for axis in axes]

    def index(place):
        at = 0
        for i, n in zip(place, sizes, strict=True):
            at = at * n + i % n
        return at

    places = itertools.product(*(range(n) for n in sizes))
    pairs = [(index(place), index([i + 1 for i in place])) for place in places]
    return lax.ppermute(value, axes, pairs)


def exchange(buf, axis):
    n = lax.axis_size(axis)
    rows, lanes = buf.shape
    got = lax.all_to_all(buf.reshape(n, 1, rows * lanes // n), axis, 0, 0, tiled=True)
    return got.reshape(rows, lanes)


def interfaces(buf, axis, lines, halves, count):
    n = lax.axis_size(axis)
    m = lines // n
    every = exchange(buf, axis)
    kernel = functools.partial(solve_kernel, n, m, halves, count)
    (ends,) = call(kernel, [every], [(n * m * 2 * halves, LANES)], "solve_" + axis)
    return exchange(ends, axis)


def shards(field, cond_x, cond_y, cross_weight):
    shape = nx, ny, nz = field.shape
    halves = nz // LANES
    x_plane = (ny, nz)
    y_plane = (nx, nz)
    blocks = pltpu.SemaphoreType.DMA((ny // SUB,))
    single = [tile_rows(v).reshape(nx, ny * halves, 1, LANES) for v in (field, cross_weight, cond_x)]
    (rows,) = call(
        functools.partial(pack_kernel, ny), single, [(4 * halves * nx, 1, LANES)], "pack",
        scratch=(pltpu.SemaphoreType.DMA((4 * halves,)),), hbm_args=(0, 1, 2), limit=MOST_VMEM,
    )
    rows = from_before(rows, "gy").reshape(4 * halves * nx, LANES)
    up, corner = call(
        ahead_kernel, [field, cross_weight, cond_x], [(4, *x_plane), (SUB, nz)], "ahead"
    )
    corner = from_before(corner, "gx", "gy")
    got = from_before(up, "gx")
    gam_x, tau_x, phi_x, mat_x, side = call(
        forward_x_kernel, [field, cross_weight, cond_x, rows, up],
        [(nx - 1, *x_plane)] * 3 + [(3, *x_plane), (4, *x_plane)], "forward_x",
    )
    (turned,) = call(
        functools.partial(turn_kernel, shape), [tile_rows(cond_y)], [(ny, *y_plane)], "turn"
    )
    buf_x, extra = call(
        finish_x_kernel, [got, corner, mat_x, side, turned],
        [(ny * 4 * halves, LANES), x_plane], "finish_x",
    )
    ends_x = interfaces(buf_x, "gx", ny, halves, 4)
    phi_y, gam_y, tau_y, buf_y = call(
        functools.partial(middle_kernel, shape),
        [ends_x, extra, phi_x, gam_x, tau_x, turned],
        [(ny - 1, *y_plane)] * 3 + [(nx * 5 * halves, LANES)], "middle",
        scratch=(y_scratch(shape),),
    )
    ends_y = interfaces(buf_y, "gy", nx, halves, 5)
    (out,) = call(
        functools.partial(backward_y_kernel, shape), [ends_y, phi_y, gam_y, tau_y],
        [(nx, ny // SUB, SUB * halves, LANES)], "backward_y",
        scratch=(y_scratch(shape), blocks), hbm_outs=(0,),
    )
    return from_y_blocks(out, shape)


def solution(mesh):
    spec = P("gx", "gy", None)
    return jax.shard_map(
        shards, mesh=mesh, in_specs=(spec,) * 4, out_specs=spec, check_vma=False
    )
```

```python
import functools
import itertools

import jax
import jax.numpy as jnp
from jax import lax
from jax.experimental import pallas as pl
from jax.experimental.pallas import tpu as pltpu
from jax.sharding import PartitionSpec as P

STEP = 16384.0
LANES = 128
SPARE = 8
SUB = 8
MIB = 1 << 20
MOST_VMEM = 55574528
f32 = jnp.float32


def tile_rows(x):
    nx, ny, nz = x.shape
    x = x.reshape(nx, ny // SUB, SUB, nz // LANES, LANES)
    return x.transpose(0, 1, 3, 2, 4).reshape(nx * ny * nz // LANES, LANES)


def from_y_blocks(v, shape):
    nx, ny, nz = shape
    v = v.reshape(nx, ny // SUB, nz // LANES, SUB, LANES)
    return v.transpose(0, 1, 3, 2, 4).reshape(nx, ny, nz)


def y_scratch(shape):
    nx, ny, nz = shape
    return pltpu.VMEM((ny // SUB, nx * (nz * SUB // LANES + SPARE), LANES), f32)


def y_rows(shape, y, h):
    nx, _, nz = shape
    return y // SUB, pl.ds(h * SUB + y % SUB, nx, stride=SUB * nz // LANES + SPARE), slice(None)


def load_y(ref, shape, y):
    return jnp.concatenate([ref[y_rows(shape, y, h)] for h in range(shape[2] // LANES)], axis=1)


def load_y_whole(ref, shape, y):
    nx, ny, nz = shape
    at = y // SUB * SUB * (nz // LANES) + y % SUB
    parts = [
        ref[pl.ds(at + h * SUB, nx, stride=ny * nz // LANES), :] for h in range(nz // LANES)
    ]
    return jnp.concatenate(parts, axis=1)


def store_y(ref, shape, y, value):
    for h in range(shape[2] // LANES):
        ref[y_rows(shape, y, h)] = value[:, h * LANES : (h + 1) * LANES]


def store_plane(ref, shape, x, value):
    _, ny, nz = shape
    halves = nz // LANES
    for yb in range(ny // SUB):
        for h in range(halves):
            start = x * (halves * SUB + SPARE) + h * SUB
            ref[yb, start : start + SUB, :] = value[
                yb * SUB : (yb + 1) * SUB, h * LANES : (h + 1) * LANES
            ]


def y_block_out(scratch, hbm, yb, sem):
    rows = hbm.shape[2]
    block = scratch.at[yb].reshape(hbm.shape[0], rows + SPARE, LANES).at[:, pl.ds(0, rows)]
    return pltpu.make_async_copy(block, hbm.at[:, yb], sem.at[yb])


def store_values(ref, values):
    lines, width = values[0].shape
    halves = width // LANES
    for k, value in enumerate(values):
        for h in range(halves):
            ref[pl.ds(k * halves + h, lines, stride=len(values) * halves), :] = value[
                :, h * LANES : (h + 1) * LANES
            ]


def load_values(ref, lines, count, halves):
    return [
        jnp.concatenate(
            [ref[pl.ds(k * halves + h, lines, stride=count * halves), :] for h in range(halves)],
            axis=1,
        )
        for k in range(count)
    ]


def pack_kernel(ny, field_hbm, weight_hbm, c_hbm, rows_ref, sem):
    nx, per_x = field_hbm.shape[0], field_hbm.shape[1]
    halves = per_x // ny
    copies = []
    for k, (hbm, y) in enumerate(
        ((field_hbm, ny - 1), (field_hbm, ny - 2), (weight_hbm, ny - 1), (c_hbm, ny - 1))
    ):
        for h in range(halves):
            at = (y // SUB * halves + h) * SUB + y % SUB
            place = k * halves + h
            copies.append(
                pltpu.make_async_copy(
                    hbm.at[:, at], rows_ref.at[pl.ds(place * nx, nx)], sem.at[place]
                )
            )
    for copy in copies:
        copy.start()
    for copy in copies:
        copy.wait()


def not_first(axis):
    return jnp.where(lax.axis_index(axis) == 0, 0.0, 1.0).astype(f32)


class Rows:
    def __init__(self, shape, rows_ref, inside):
        self.nx, self.n = shape[:2]
        self.row = lax.broadcasted_iota(jnp.int32, shape[1:], 0)
        self.rows_ref = rows_ref
        self.inside = inside

    def put(self, place, row, plane):
        return jnp.where(self.row == place, row, plane)

    def got(self, k, i):
        halves = self.row.shape[1] // LANES
        at = [(k * halves + h) * self.nx + i for h in range(halves)]
        return jnp.concatenate([self.rows_ref[r : r + 1, :] for r in at], axis=1)

    def plane(self, ref, k, i):
        return self.put(self.n - 1, self.got(k, i), ref[i])

    def difference(self, ref, i):
        n = self.n
        plane = ref[i]
        up = pltpu.roll(plane, n - 1, 0)
        up = self.put(n - 1, up * self.inside, up)
        down = pltpu.roll(plane, 1, 0)
        down = self.put(0, self.got(0, i) * self.inside, down)
        return up - self.put(n - 1, self.got(1, i), down)


def ahead_kernel(field_ref, weight_ref, c_ref, up_ref, corner_ref):
    n, ny, _ = c_ref.shape
    inside = not_first("gy")
    row = lax.broadcasted_iota(jnp.int32, c_ref.shape[1:], 0)
    edge = (row == 0) | (row == ny - 1)

    def difference(plane):
        up = pltpu.roll(plane, ny - 1, 0)
        up = jnp.where(row == ny - 1, up * inside, up)
        return up - jnp.where(edge, 0.0, pltpu.roll(plane, 1, 0))

    last, before = field_ref[n - 1], field_ref[n - 2]
    weight = weight_ref[n - 1] * 0.25
    before_difference = difference(before)
    up_ref[0] = difference(last)
    up_ref[1] = jnp.where(row == ny - 1, before_difference, last - weight * before_difference)
    up_ref[2] = weight
    t = STEP * c_ref[0]
    ground = jnp.ones_like(t)
    both = t + ground
    for i in range(n - 1):
        c = STEP * c_ref[i + 1]
        gam = c / (both + c)
        ground = 1.0 + gam * ground
        both = 1.0 + gam * both
        t = t * gam
    ground = ground + t * (1.0 - not_first("gx"))
    up_ref[3] = ground
    for k, (plane, y) in enumerate(
        ((last, -1), (last, -2), (before, -1), (before, -2), (weight, -1), (ground, -1))
    ):
        corner_ref[k : k + 1, :] = plane[ny + y : ny + y + 1, :]
    corner_ref[6:8, :] = jnp.zeros_like(corner_ref[6:8, :])


def forward_x_kernel(
    field_ref, weight_ref, c_ref, rows_ref, up_ref, gam_ref, tau_ref, phi_ref, mat_ref, side_ref,
):
    n = c_ref.shape[0]
    rows = Rows(c_ref.shape, rows_ref, not_first("gy"))
    left = STEP * rows.plane(c_ref, 3, 0)
    t = left
    a = jnp.zeros_like(t)
    ground = jnp.ones_like(t)
    both = t + ground
    diffs = {-1: 0.0, 0: rows.difference(field_ref, 0)}
    side_ref[3] = diffs[0]
    q = j = 0.0
    for i in range(n - 1):
        c = STEP * rows.plane(c_ref, 3, i + 1)
        inv = 1.0 / (both + c)
        gam = c * inv
        tau = t * inv
        gam_ref[i] = gam
        tau_ref[i] = tau
        a = a + tau * ground
        ground = 1.0 + gam * ground
        both = 1.0 + gam * both
        t = t * gam
        diffs[i + 1] = rows.difference(field_ref, i + 1)
        weight = rows.plane(weight_ref, 2, i) * 0.25
        if i == 0:
            side_ref[2] = weight
        h = rows.plane(field_ref, 0, i) + weight * (diffs[i + 1] - diffs.pop(i - 1)) + q
        phi_ref[i] = inv * h
        q = gam * h
        j = j + tau * h
    side_ref[0] = j
    side_ref[1] = q
    for k, value in enumerate((t, a, left)):
        mat_ref[k] = value


def finish_x_kernel(got_ref, corner_ref, mat_ref, side_ref, turned_ref, buf_ref, extra_ref):
    ny = got_ref.shape[1]
    inside_x, inside_y = not_first("gx"), not_first("gy")
    row = lax.broadcasted_iota(jnp.int32, got_ref.shape[1:], 0)
    first, last = row == 0, row == ny - 1
    f, f2, b, b2, w, ground = (corner_ref[k : k + 1, :] for k in range(6))
    difference = got_ref[0] - jnp.where(first, f * inside_y, jnp.where(last, f2, 0.0))
    weight = jnp.where(last, w, got_ref[2])
    partial = got_ref[1]
    partial = jnp.where(
        last,
        f - w * (partial - b2),
        partial + jnp.where(first, weight * (b * inside_y), 0.0),
    )
    grounds = jnp.where(last, ground, got_ref[3])
    t, a, left = (mat_ref[k] for k in range(3))
    f0 = side_ref[2] * difference * -inside_x
    extra = f0 / left
    source = partial + weight * side_ref[3] * inside_x
    j = (side_ref[0] + f0 - (a + t) * extra) * inside_x + source
    q = side_ref[1] + t * extra
    extra_ref[...] = extra
    store_values(buf_ref, [t * inside_x, grounds + a * inside_x, j, q])


def solve_kernel(n, m, halves, count, in_ref, out_ref):
    stride = m * count * halves

    def get(k):
        return jnp.concatenate(
            [
                in_ref[pl.ds((l * count + k) * halves + h, n, stride=stride), :]
                for l in range(m)
                for h in range(halves)
            ],
            axis=1,
        )

    def after(v, d=1):
        return pltpu.roll(v, n - d, 0)

    def before(v, d=1):
        return pltpu.roll(v, d, 0)

    low, g, j, q, *ground = (get(k) for k in range(count))
    g = after(g)
    if ground:
        g = g + ground[0]
    high = after(low)
    r = q + after(j)
    d = 1
    while d < n:
        inv = 1.0 / (g + low + high)
        gi = g * inv
        ri = r * inv
        g, r, low, high = (
            g + low * before(gi, d) + high * after(gi, d),
            r + low * before(ri, d) + high * after(ri, d),
            low * before(low * inv, d),
            high * after(high * inv, d),
        )
        d *= 2
    u = r / g
    u_prev = before(u)
    for l in range(m):
        for k, value in enumerate((u_prev, u)):
            for h in range(halves):
                at = (l * halves + h) * LANES
                out_ref[pl.ds((l * 2 + k) * halves + h, n, stride=m * 2 * halves), :] = value[
                    :, at : at + LANES
                ]


def backward(n, u_prev, u_own, gam_ref, tau_ref, phi_ref, emit):
    u = u_own
    emit(n - 1, u)
    for i in range(n - 2, -1, -1):
        u = (phi_ref[i] + tau_ref[i] * u_prev) + gam_ref[i] * u
        emit(i, u)


def turn_kernel(shape, c_ref, out_ref):
    for y in range(shape[1]):
        out_ref[y] = STEP * load_y_whole(c_ref, shape, y)


def middle_kernel(
    shape, ends_ref, extra_ref, phi_x_ref, gam_x_ref, tau_x_ref, c_ref,
    phi_ref, gam_ref, tau_ref, buf_ref, half_ref,
):
    nx, ny, nz = shape
    u_prev, u_own = load_values(ends_ref, ny, 2, nz // LANES)
    backward(nx, u_prev * not_first("gx") + extra_ref[...], u_own, gam_x_ref, tau_x_ref, phi_x_ref,
             lambda i, u: store_plane(half_ref, shape, i, u))
    t = c_ref[0]
    a = jnp.zeros_like(t)
    ground = jnp.ones_like(t)
    both = t + ground
    q = j = 0.0
    for y in range(ny - 1):
        c = c_ref[y + 1]
        h = load_y(half_ref, shape, y) + q
        inv = 1.0 / (both + c)
        gam = c * inv
        tau = t * inv
        phi_ref[y] = inv * h
        gam_ref[y] = gam
        tau_ref[y] = tau
        q = gam * h
        j = j + tau * h
        a = a + tau * ground
        ground = 1.0 + gam * ground
        both = 1.0 + gam * both
        t = t * gam
    inside = not_first("gy")
    j = j * inside + load_y(half_ref, shape, ny - 1)
    store_values(buf_ref, [t * inside, a * inside, j, q, ground + t * (1.0 - inside)])


def backward_y_kernel(shape, ends_ref, phi_ref, gam_ref, tau_ref, out_hbm, out_ref, sem):
    nx, ny, nz = shape
    u_prev, u_own = load_values(ends_ref, nx, 2, nz // LANES)
    copies = []

    def emit(y, u):
        store_y(out_ref, shape, y, u)
        if y % SUB == 0:
            copies.append(y_block_out(out_ref, out_hbm, y // SUB, sem))
            copies[-1].start()

    backward(ny, u_prev * not_first("gy"), u_own, gam_ref, tau_ref, phi_ref, emit)
    for copy in copies:
        copy.wait()


IN_VMEM = pl.BlockSpec(memory_space=pltpu.VMEM)
IN_PLACE = pl.BlockSpec(memory_space=pl.ANY)


def call(kernel, args, outs, name, scratch=(), hbm_args=(), hbm_outs=(), bytes_accessed=1 << 20,
         limit=16 * MIB):
    return pl.pallas_call(
        kernel,
        out_shape=[jax.ShapeDtypeStruct(s, f32) for s in outs],
        in_specs=[IN_PLACE if k in hbm_args else IN_VMEM for k in range(len(args))],
        out_specs=[IN_PLACE if k in hbm_outs else IN_VMEM for k in range(len(outs))],
        scratch_shapes=list(scratch),
        compiler_params=pltpu.CompilerParams(vmem_limit_bytes=limit),
        cost_estimate=pl.CostEstimate(flops=1 << 20, bytes_accessed=bytes_accessed, transcendentals=0),
        name=name,
    )(*args)


def from_before(value, *axes):
    sizes = [lax.axis_size(axis) for axis in axes]

    def index(place):
        at = 0
        for i, n in zip(place, sizes, strict=True):
            at = at * n + i % n
        return at

    places = itertools.product(*(range(n) for n in sizes))
    pairs = [(index(place), index([i + 1 for i in place])) for place in places]
    return lax.ppermute(value, axes, pairs)


def exchange(buf, axis):
    n = lax.axis_size(axis)
    rows, lanes = buf.shape
    got = lax.all_to_all(buf.reshape(n, 1, rows * lanes // n), axis, 0, 0, tiled=True)
    return got.reshape(rows, lanes)


def interfaces(buf, axis, lines, halves, count):
    n = lax.axis_size(axis)
    m = lines // n
    every = exchange(buf, axis)
    kernel = functools.partial(solve_kernel, n, m, halves, count)
    (ends,) = call(kernel, [every], [(n * m * 2 * halves, LANES)], "solve_" + axis)
    return exchange(ends, axis)


def shards(field, cond_x, cond_y, cross_weight):
    shape = nx, ny, nz = field.shape
    halves = nz // LANES
    x_plane = (ny, nz)
    y_plane = (nx, nz)
    blocks = pltpu.SemaphoreType.DMA((ny // SUB,))
    single = [tile_rows(v).reshape(nx, ny * halves, 1, LANES) for v in (field, cross_weight, cond_x)]
    (rows,) = call(
        functools.partial(pack_kernel, ny), single, [(4 * halves * nx, 1, LANES)], "pack",
        scratch=(pltpu.SemaphoreType.DMA((4 * halves,)),), hbm_args=(0, 1, 2), limit=MOST_VMEM,
    )
    rows = from_before(rows, "gy").reshape(4 * halves * nx, LANES)
    up, corner = call(
        ahead_kernel, [field, cross_weight, cond_x], [(4, *x_plane), (SUB, nz)], "ahead"
    )
    corner = from_before(corner, "gx", "gy")
    got = from_before(up, "gx")
    gam_x, tau_x, phi_x, mat_x, side = call(
        forward_x_kernel, [field, cross_weight, cond_x, rows, up],
        [(nx - 1, *x_plane)] * 3 + [(3, *x_plane), (4, *x_plane)], "forward_x",
    )
    (turned,) = call(
        functools.partial(turn_kernel, shape), [tile_rows(cond_y)], [(ny, *y_plane)], "turn"
    )
    buf_x, extra = call(
        finish_x_kernel, [got, corner, mat_x, side, turned],
        [(ny * 4 * halves, LANES), x_plane], "finish_x",
    )
    ends_x = interfaces(buf_x, "gx", ny, halves, 4)
    phi_y, gam_y, tau_y, buf_y = call(
        functools.partial(middle_kernel, shape),
        [ends_x, extra, phi_x, gam_x, tau_x, turned],
        [(ny - 1, *y_plane)] * 3 + [(nx * 5 * halves, LANES)], "middle",
        scratch=(y_scratch(shape),),
    )
    ends_y = interfaces(buf_y, "gy", nx, halves, 5)
    (out,) = call(
        functools.partial(backward_y_kernel, shape), [ends_y, phi_y, gam_y, tau_y],
        [(nx, ny // SUB, SUB * halves, LANES)], "backward_y",
        scratch=(y_scratch(shape), blocks), hbm_outs=(0,),
    )
    return from_y_blocks(out, shape)


def solution(mesh):
    spec = P("gx", "gy", None)
    return jax.shard_map(
        shards, mesh=mesh, in_specs=(spec,) * 4, out_specs=spec, check_vma=False
    )
```
